128 devices in a mesh: dp: 8 (over x, z_hi), seq: 16 (over y, z_lo, core).
Axes of the slice: x: 4, y: 4, z: 4 (z_hi: 2, z_lo: 2; z = z_hi * 2 + z_lo), core: 2. Of those that a mesh axis runs over, the one named last changes fastest.
Arguments:
- tokens: int32 [65536], P(('dp', 'seq')), parts along dimension 0, may hold values from 0 to 3
- dilations: int32 [2], replicated, may hold values from 1 to 64, as said below
- embed: float32 [4, 256], replicated, may hold values from -6 to 6
- conv_weight: float32 [2, 3, 256, 512], replicated, may hold values from -0.1875 to 0.1875
- mix_weight: float32 [2, 256, 512], replicated, may hold values from -0.1875 to 0.1875
- gate_bias: float32 [2, 512], replicated, may hold values from -3 to 3
- out_weight: float32 [2, 256, 256], replicated, may hold values from -0.375 to 0.375
- cot_fwd: float32 [65536, 256], P(('dp', 'seq')), parts along dimension 0, may hold values from -6 to 6
- cot_rev: float32 [65536, 256], P(('dp', 'seq')), parts along dimension 0, may hold values from -6 to 6
Outputs:
- out_fwd: float32 [65536, 256], P(('dp', 'seq')), parts along dimension 0
- out_rev: float32 [65536, 256], P(('dp', 'seq')), parts along dimension 0
- grad_embed: float32 [32, 256], P('dp'), parts along dimension 0
- grad_conv: float32 [16, 3, 256, 512], P('dp'), parts along dimension 0
- grad_mix: float32 [16, 256, 512], P('dp'), parts along dimension 0
- grad_bias: float32 [16, 512], P('dp'), parts along dimension 0
- grad_out: float32 [16, 256, 256], P('dp'), parts along dimension 0
The draws below stay inside these ranges and needn't reach their ends.
There are 8 independent parts, one for each index of `dp`. The reference program is written for one: setup_inputs(seed, part) draws one part's arguments, and reference() takes and returns one part's arrays. A program takes and returns all parts, laid end to end along the dimension named above; an argument that names none is the same for every part. Nothing has to cross between parts.
Inputs may be any that keep to these rules, and one draw needn't show every extreme that they name: `dilations`: exactly one layer's dilation equals 64; the others lie below it.
All inputs are finite; a program needn't handle non-finite values.
Results may differ from the reference program's by a relative error of at most 0.00012.
Values sent between devices are 32-bit elements; how exact they have to be, the bound alone decides.
A program may use at most 128 MiB of HBM per device.

```python
import jax
import jax.numpy as jnp
from jax import lax

HALF = 256
LAYERS = 2
DMAX = 64
SEQLEN = 8192


def draw_dilations(key, part):
    values = jax.random.randint(key, (LAYERS,), 1, DMAX)
    chosen = jax.random.randint(jax.random.fold_in(key, 7), (), 0, LAYERS)
    return jnp.where(jnp.arange(LAYERS) == chosen, DMAX, values).astype(jnp.int32)


def touch_ends(entries, stream_key, low, top_value):
    index_at = [jax.random.randint(jax.random.fold_in(stream_key, axis), (), 0, length) for axis, length in enumerate(entries.shape)]
    longest = entries.shape.index(max(entries.shape))
    neighbour = index_at[:longest] + [(index_at[longest] + 1) % entries.shape[longest]] + index_at[longest + 1:]
    return entries.at[tuple(index_at)].set(low).at[tuple(neighbour)].set(top_value)


def steps_of(own_key, dims, cuts, least, high):
    level, own = 1.0, jax.random.fold_in(own_key, 6)
    for axis_at, parts in cuts:
        heights = jnp.exp(jax.random.uniform(jax.random.fold_in(own, axis_at), (parts,), jnp.float32, least / len(cuts), high / len(cuts)))
        level = level * jnp.repeat(heights, dims[axis_at] // parts).reshape([-1 if axis == axis_at else 1 for axis in range(len(dims))])
    return level


def centred(own_key, shape, deviation, most, cuts=(), kind=jnp.bfloat16):
    drawn = deviation * jax.random.normal(own_key, shape, jnp.float32)
    if cuts:
        drawn = drawn * steps_of(own_key, shape, cuts, -0.22, 0.18)
    return jnp.clip(drawn, -most, most).astype(kind)


def setup_inputs(seed: int = 0, part: int = 0) -> dict:
    seeds = jax.random.split(jax.random.key(seed), 10)
    own_keys = jax.random.split(jax.random.fold_in(seeds[9], part), 10)
    return {
        "tokens": touch_ends(jax.random.randint(own_keys[0], (SEQLEN,), 0, 4), jax.random.fold_in(own_keys[0], 1), 0, 3).astype(jnp.int32),
        "dilations": draw_dilations(jax.random.fold_in(seeds[9], 71), part),
        "embed": centred(seeds[2], (4, HALF), 1.0, 6.0, (), jnp.float32),
        "conv_weight": centred(seeds[3], (LAYERS, 3, HALF, 2 * HALF), (4 * HALF) ** -0.5, 0.1875, (), jnp.float32),
        "mix_weight": centred(seeds[4], (LAYERS, HALF, 2 * HALF), (4 * HALF) ** -0.5, 0.1875, (), jnp.float32),
        "gate_bias": centred(seeds[5], (LAYERS, 2 * HALF), 0.5, 3.0, (), jnp.float32),
        "out_weight": centred(seeds[6], (LAYERS, HALF, HALF), HALF ** -0.5, 0.375, (), jnp.float32),
        "cot_fwd": centred(own_keys[7], (SEQLEN, HALF), 1.0, 6.0, ((0, 16),), jnp.float32),
        "cot_rev": centred(own_keys[8], (SEQLEN, HALF), 1.0, 6.0, ((0, 16),), jnp.float32),
    }


def stencil_rows(padded, dilation, length):
    pieces = []
    for offset in range(3):
        begin = (DMAX + (offset - 1) * dilation).astype(jnp.int32)
        pieces.append(lax.dynamic_slice_in_dim(padded, begin, length, 0))
    return jnp.concatenate(pieces, axis=1)

def strand_layer(own, partner, dilation, conv_piece, mix_piece, bias_piece, out_piece):
    length, channels = own.shape
    padded = jnp.pad(own, ((DMAX, DMAX), (0, 0)))
    inputs = jnp.concatenate([stencil_rows(padded, dilation, length), partner], axis=1)
    joined = jnp.concatenate([conv_piece.reshape(3 * channels, 2 * channels), mix_piece], axis=0)
    mixed_rows = jnp.dot(inputs, joined, precision=lax.Precision.HIGHEST, preferred_element_type=jnp.float32) + bias_piece
    hidden = jnp.tanh(mixed_rows[:, :channels]) * jax.nn.sigmoid(mixed_rows[:, channels:])
    return own + jnp.dot(hidden, out_piece, precision=lax.Precision.HIGHEST, preferred_element_type=jnp.float32)

def reference(tokens, dilations, embed, conv_weight, mix_weight, gate_bias, out_weight, cot_fwd, cot_rev):

    def forward(embed_table, conv_all, mix_all, bias_all, out_all):
        strand_fwd = jnp.take(embed_table, tokens, axis=0)
        strand_rev = jnp.flip(jnp.take(embed_table, 3 - tokens, axis=0), 0)
        for layer_at in range(LAYERS):
            partner_fwd = jnp.flip(strand_rev, 0)
            partner_rev = jnp.flip(strand_fwd, 0)
            dilation = dilations[layer_at].astype(jnp.int32)
            new_fwd = strand_layer(strand_fwd, partner_fwd, dilation, conv_all[layer_at], mix_all[layer_at], bias_all[layer_at], out_all[layer_at])
            new_rev = strand_layer(strand_rev, partner_rev, dilation, conv_all[layer_at], mix_all[layer_at], bias_all[layer_at], out_all[layer_at])
            strand_fwd, strand_rev = (new_fwd, new_rev)
        return (strand_fwd, strand_rev)
    outputs, pullback = jax.vjp(forward, embed, conv_weight, mix_weight, gate_bias, out_weight)
    gradients = pullback((cot_fwd, cot_rev))
    return (outputs[0], outputs[1], gradients[0], gradients[1], gradients[2], gradients[3], gradients[4])
```

```python
import jax
import jax.numpy as jnp
import numpy as np
from jax import lax
from jax.sharding import PartitionSpec as P

LAYERS = 2
DMAX = 64
ROWS = 104
HIGH = lax.Precision.HIGH
EXACT = lax.Precision.HIGHEST


def selectors():
    row = np.arange(ROWS)
    left, own, right = row // 20, (row // 5) % 4, row % 5
    live = row < 100
    base = np.arange(4)
    pick_left = ((left[:, None] == base) & live[:, None]).astype(np.float32)
    pick_own = ((own[:, None] == base) & live[:, None]).astype(np.float32)
    pick_right = ((right[:, None] == base) & live[:, None]).astype(np.float32)
    flipped = np.array([3, 2, 1, 0, 4, 0])
    other = np.where(live, flipped[right] * 20 + flipped[own] * 5 + flipped[left], row)
    swap = (other[:, None] == row).astype(np.float32)
    return pick_left, pick_own, pick_right, pick_own[:, ::-1].copy(), swap


def dot(a, b, precision=EXACT):
    return jnp.dot(a, b, precision=precision, preferred_element_type=jnp.float32)


def dot_t(a, b, precision=EXACT):
    return lax.dot_general(
        a, b, (((0,), (0,)), ((), ())), precision=precision, preferred_element_type=jnp.float32
    )


def dot_nt(a, b, precision=EXACT):
    return lax.dot_general(
        a, b, (((1,), (1,)), ((), ())), precision=precision, preferred_element_type=jnp.float32
    )


def rows_at(sequence, begin, length, dilations):
    window = lax.dynamic_slice_in_dim(sequence, begin, length + 4 * DMAX, 0)
    span = length + 2 * DMAX
    own = lax.slice_in_dim(window, DMAX, DMAX + span)
    left = lax.dynamic_slice_in_dim(window, DMAX - dilations[0], span, 0)
    right = lax.dynamic_slice_in_dim(window, DMAX + dilations[0], span, 0)
    code = jnp.where(own == 4, 127, left * 20 + own * 5 + right)
    return [
        lax.dynamic_slice_in_dim(code, DMAX + step * dilations[1], length, 0) for step in (-1, 0, 1)
    ]


def on_device(
    tokens, dilations, embed, conv_weight, mix_weight, gate_bias, out_weight, cot_fwd, cot_rev
):
    length = tokens.shape[0]
    half = embed.shape[1]
    sel_left, sel_own, sel_right, sel_comp, swap = [jnp.asarray(s) for s in selectors()]
    whole = lax.all_gather(tokens, "seq", tiled=True)
    begin = lax.axis_index("seq") * length
    codes = []
    for strand in (whole, jnp.flip(3 - whole)):
        codes.append(rows_at(jnp.pad(strand, 2 * DMAX, constant_values=4), begin, length, dilations))
    level = jnp.arange(ROWS, dtype=jnp.int32)
    hots = [
        (jnp.concatenate([codes[0][at], codes[1][at]])[:, None] == level).astype(jnp.float32)
        for at in range(3)
    ]

    mixed = gate_bias[0] * jnp.ones((ROWS, 1), jnp.float32)
    weights = [conv_weight[0, 0], conv_weight[0, 1], conv_weight[0, 2], mix_weight[0]]
    picks = [sel_left, sel_own, sel_right, sel_comp]
    for pick, weight in zip(picks, weights):
        mixed = mixed + dot(pick, dot(embed, weight))
    tanh_0 = jnp.tanh(mixed[:, :half])
    sig_0 = jax.nn.sigmoid(mixed[:, half:])
    hidden_0 = tanh_0 * sig_0
    table = dot(sel_own, embed) + dot(hidden_0, out_weight[0])
    table_left = dot(table, conv_weight[1, 0])
    table_own = dot(table, conv_weight[1, 1]) + dot(dot(swap, table), mix_weight[1]) + gate_bias[1]
    table_right = dot(table, conv_weight[1, 2])

    hot = jnp.concatenate(hots, axis=1)
    mixed = dot(hot, jnp.concatenate([table_left, table_own, table_right], axis=0), HIGH)
    tanh_1 = jnp.tanh(mixed[:, :half])
    sig_1 = jax.nn.sigmoid(mixed[:, half:])
    hidden_1 = tanh_1 * sig_1
    result = dot(hots[1], table, HIGH) + dot(hidden_1, out_weight[1], HIGH)

    cot = jnp.concatenate([cot_fwd, cot_rev], axis=0)
    grad_hidden = dot_nt(cot, out_weight[1], HIGH)
    grad_mixed = jnp.concatenate(
        [
            grad_hidden * sig_1 * (1.0 - tanh_1 * tanh_1),
            grad_hidden * tanh_1 * sig_1 * (1.0 - sig_1),
        ],
        axis=1,
    )
    sums = dot_t(hot, grad_mixed, HIGH)
    cot_sums = dot_t(hots[1], cot, HIGH)
    out_1 = dot_t(hidden_1, cot, HIGH)
    total = lax.psum(
        jnp.concatenate([sums.reshape(-1, half), cot_sums, out_1], axis=0), "seq"
    )
    sums = total[: 6 * ROWS].reshape(3 * ROWS, 2 * half)
    cot_sums = total[6 * ROWS : 7 * ROWS]
    out_1 = total[7 * ROWS :]

    sum_left, sum_own, sum_right = sums[:ROWS], sums[ROWS : 2 * ROWS], sums[2 * ROWS :]
    sum_other = dot(swap, sum_own)
    conv_1 = jnp.stack([dot_t(table, part) for part in (sum_left, sum_own, sum_right)])
    mix_1 = dot_t(table, sum_other)
    bias_1 = jnp.sum(sum_own, axis=0)
    grad = (
        cot_sums
        + dot_nt(sum_left, conv_weight[1, 0])
        + dot_nt(sum_own, conv_weight[1, 1])
        + dot_nt(sum_right, conv_weight[1, 2])
        + dot_nt(sum_other, mix_weight[1])
    )
    out_0 = dot_t(hidden_0, grad)
    grad_hidden = dot_nt(grad, out_weight[0])
    grad_mixed = jnp.concatenate(
        [
            grad_hidden * sig_0 * (1.0 - tanh_0 * tanh_0),
            grad_hidden * tanh_0 * sig_0 * (1.0 - sig_0),
        ],
        axis=1,
    )
    bias_0 = jnp.sum(grad_mixed, axis=0)
    grad_embed = dot_t(sel_own, grad)
    pieces = []
    for pick, weight in zip(picks, weights):
        part = dot_t(pick, grad_mixed)
        pieces.append(dot_t(embed, part))
        grad_embed = grad_embed + dot_nt(part, weight)
    return (
        result[:length],
        result[length:],
        grad_embed,
        jnp.stack([jnp.stack(pieces[:3]), conv_1]),
        jnp.stack([pieces[3], mix_1]),
        jnp.stack([bias_0, bias_1]),
        jnp.stack([out_0, out_1]),
    )


def solution(mesh):
    in_specs = (
        P(("dp", "seq")),
        P(),
        P(),
        P(),
        P(),
        P(),
        P(),
        P(("dp", "seq"), None),
        P(("dp", "seq"), None),
    )
    out_specs = (
        P(("dp", "seq"), None),
        P(("dp", "seq"), None),
        P("dp", None),
        P("dp", None, None, None),
        P("dp", None, None),
        P("dp", None),
        P("dp", None, None),
    )
    return jax.shard_map(
        on_device, mesh=mesh, in_specs=in_specs, out_specs=out_specs, check_vma=False
    )
```

```python
import functools

import jax
import jax.numpy as jnp
import numpy as np
from jax import lax
from jax.experimental import pallas as pl
from jax.experimental.pallas import tpu as pltpu
from jax.sharding import PartitionSpec as P

MESH = pl.DeviceIdType.MESH
ROWS = 128
KEPT = 104
HALF = 256
PIECE = 64
OUTSIDE = 4
NONE = 255
F32 = jnp.float32
BF16 = jnp.bfloat16
VMEM = pl.BlockSpec(memory_space=pltpu.VMEM)
SMEM = pl.BlockSpec(memory_space=pltpu.SMEM)


def selectors():
    row = np.arange(ROWS)
    live = row < 100
    left, own, right = row // 20, (row // 5) % 4, row % 5
    picks = np.zeros((ROWS, 16), np.float32)
    for base in range(4):
        picks[:, base] = live & (left == base)
        picks[:, 4 + base] = live & (own == base)
        picks[:, 8 + base] = live & (right == base)
        picks[:, 12 + base] = live & (own == 3 - base)
    flipped = np.array([3, 2, 1, 0, 4, 0, 0])
    other = np.where(live, flipped[right] * 20 + flipped[own] * 5 + flipped[left], row)
    swap = (other[:, None] == row).astype(np.float32)
    return picks, picks.T.copy(), swap


def split(value):
    high = value.astype(BF16)
    return high, (value - high.astype(F32)).astype(BF16)


def dot(a, b, dims=((1,), (0,))):
    return lax.dot_general(a, b, (dims, ((), ())), preferred_element_type=F32)


def dot2(exact, parts, dims=((1,), (0,))):
    return dot(exact, parts[0], dims) + dot(exact, parts[1], dims)


def dot3(a, b, dims=((1,), (0,))):
    return dot(a[0], b[0], dims) + (dot(a[0], b[1], dims) + dot(a[1], b[0], dims))


NT = ((1,), (1,))
TN = ((0,), (0,))


def sigmoid(value):
    return 0.5 * jnp.tanh(0.5 * value) + 0.5


def exclusive(value, bits):
    total = 0
    for bit in (1, 2, 4):
        digit = lax.rem(lax.div(value, bit), 2)
        total = total + bit * (1 - digit if bits & bit else digit)
    return total


def token_kernel(count, tokens_ref, all_ref, landed, sems):
    me = lax.axis_index("seq")
    barrier = pltpu.get_barrier_semaphore()
    peers = [lax.rem(me + step, count) for step in range(1, count)]
    for peer in peers:
        pl.semaphore_signal(barrier, inc=1, device_id={"seq": peer}, device_id_type=MESH)
    pl.semaphore_wait(barrier, count - 1)
    copies = []
    for step, peer in enumerate(peers):
        copies.append(
            pltpu.make_async_remote_copy(
                src_ref=tokens_ref,
                dst_ref=landed.at[me],
                send_sem=sems.at[0, step],
                recv_sem=sems.at[1, step],
                device_id={"seq": peer},
                device_id_type=MESH,
            )
        )
        copies[-1].start()
    edge = jnp.full(tokens_ref.shape, OUTSIDE, jnp.int32)
    all_ref[0] = edge
    all_ref[count + 1] = edge
    all_ref[me + 1] = tokens_ref[...]
    for copy in copies:
        copy.wait_recv()
    for step in range(1, count):
        source = lax.rem(me + step, count)
        all_ref[source + 1] = landed[source]
    for copy in copies:
        copy.wait_send()


def gather_tokens(tokens, count):
    return pl.pallas_call(
        functools.partial(token_kernel, count),
        out_shape=jax.ShapeDtypeStruct((count + 2,) + tokens.shape, jnp.int32),
        in_specs=[VMEM],
        out_specs=VMEM,
        scratch_shapes=[
            pltpu.VMEM((count,) + tokens.shape, jnp.int32),
            pltpu.SemaphoreType.DMA((2, count - 1)),
        ],
        compiler_params=pltpu.CompilerParams(collective_id=0, has_side_effects=True),
        name="gather_tokens",
    )(tokens)


def shifted(rows, amount, sign):
    lane = lax.broadcasted_iota(jnp.int32, (1, 128), 1)
    turned = [pltpu.roll(row, 128 - amount if sign > 0 else amount, 1) for row in rows]
    result = []
    for at in range(len(rows)):
        if sign > 0:
            beside = turned[min(at + 1, len(rows) - 1)]
            result.append(jnp.where(lane < 128 - amount, turned[at], beside))
        else:
            beside = turned[max(at - 1, 0)]
            result.append(jnp.where(lane >= amount, turned[at], beside))
    return result


def row_codes(rows, near, far, mirrored):
    left, right = shifted(rows, near, -1), shifted(rows, near, 1)
    codes = []
    for lower, own, upper in zip(left, rows, right):
        if mirrored:
            lower, upper = upper, lower
            lower = jnp.where(lower == OUTSIDE, OUTSIDE, 3 - lower)
            upper = jnp.where(upper == OUTSIDE, OUTSIDE, 3 - upper)
            code = lower * 20 + (3 - own) * 5 + upper
        else:
            code = lower * 20 + own * 5 + upper
        codes.append(jnp.where(own == OUTSIDE, NONE, code))
    before, after = shifted(codes, far, -1), shifted(codes, far, 1)
    if mirrored:
        before, after = after, before
    return before[1:5] + codes[1:5] + after[1:5]


def tables(embed_ref, conv_ref, mix_ref, bias_ref, out_ref, picks, swap, wide, high, low):
    wide[...] = jnp.zeros_like(wide)
    wide[16:20, :HALF] = embed_ref[...]
    embed = split(wide[16:24, :HALF])
    for at in range(4):
        weight = conv_ref[0, at] if at < 3 else mix_ref[0]
        wide[4 * at : 4 * at + 4, :] = dot3(embed, split(weight))[:4]
    mixed = dot2(picks, split(wide[:16, :])) + bias_ref[0:1, :]
    tanh = jnp.tanh(mixed[:, :HALF])
    sig = sigmoid(mixed[:, HALF:])
    wide[...] = jnp.zeros_like(wide)
    wide[4:8, :HALF] = embed_ref[...]
    table = dot2(picks, split(wide[:16, :HALF])) + dot3(split(tanh * sig), split(out_ref[0]))
    parts = split(table)
    swapped = [dot(swap, part).astype(BF16) for part in parts]
    weights = [split(conv_ref[1, at]) for at in range(3)]
    for at in range(3):
        product = dot3(parts, weights[at])
        if at == 1:
            product = product + dot3(swapped, split(mix_ref[1])) + bias_ref[1:2, :]
        high[ROWS * at : ROWS * at + ROWS, :], low[ROWS * at : ROWS * at + ROWS, :] = split(product)
    return table, tanh, sig


def local_kernel(
    dilations_ref,
    tokens_ref,
    embed_ref,
    conv_ref,
    mix_ref,
    bias_ref,
    out_weight_ref,
    cot_fwd_ref,
    cot_rev_ref,
    picks_ref,
    swap_ref,
    out_fwd_ref,
    out_rev_ref,
    part_ref,
    table_ref,
    tanh_ref,
    sig_ref,
    wide,
    high,
    low,
    codes,
    hot,
    hot_t,
    hidden_parts,
    cot_parts,
    grad_parts,
):
    count = tokens_ref.shape[0] - 2
    me = lax.axis_index("seq")
    near, far = dilations_ref[0], dilations_ref[1]

    table, tanh, sig = tables(
        embed_ref, conv_ref, mix_ref, bias_ref, out_weight_ref, picks_ref[...], swap_ref[...], wide, high, low
    )
    table_ref[...], tanh_ref[...], sig_ref[...] = table, tanh, sig
    table_parts = split(table)

    codes[...] = jnp.zeros_like(codes)
    for strand in range(2):
        block = me if strand == 0 else count - 1 - me
        before, own, after = tokens_ref[block], tokens_ref[block + 1], tokens_ref[block + 2]
        rows = [before[3:4]] + [own[at : at + 1] for at in range(4)] + [after[0:1]]
        for at, code in enumerate(row_codes(rows, near, far, strand == 1)):
            tap, row = at // 4, at % 4
            codes[16 * strand + 4 * tap + (row if strand == 0 else 3 - row)] = code.astype(F32)[0]
    lane = lax.broadcasted_iota(jnp.int32, (128, 128), 1)
    sub = lax.broadcasted_iota(jnp.int32, (128, 128), 0)
    level = lane.astype(F32)
    level_t = sub.astype(F32)
    for strand in range(2):
        given = codes[16 * strand : 16 * strand + 16, :].astype(BF16)
        if strand == 0:
            order = jnp.where(lane == sub, 1.0, 0.0).astype(BF16)
        else:
            order = jnp.where(lane + sub == 127, 1.0, 0.0).astype(BF16)
        across = dot(given, order)
        down = dot(order, given, NT)
        for tap in range(3):
            for row in range(4):
                at = 4 * tap + row
                position = 512 * strand + 128 * row
                hot[position : position + 128, 128 * tap : 128 * tap + 128] = jnp.where(
                    down[:, at : at + 1] == level, 1.0, 0.0
                ).astype(BF16)
                hot_t[128 * tap : 128 * tap + 128, position : position + 128] = jnp.where(
                    across[at : at + 1, :] == level_t, 1.0, 0.0
                ).astype(BF16)

    out_parts = split(out_weight_ref[1])
    for block in range(4):
        rows = pl.ds(256 * block, 256)
        inner = pl.ds(256 * (block % 2), 256)
        cot = (cot_fwd_ref if block < 2 else cot_rev_ref)[inner, :]
        chosen = hot[rows, :]
        mixed = dot2(chosen, (high[...], low[...]))
        act, gate = jnp.tanh(mixed[:, :HALF]), sigmoid(mixed[:, HALF:])
        hidden = split(act * gate)
        (out_fwd_ref if block < 2 else out_rev_ref)[inner, :] = dot2(
            chosen[:, ROWS : 2 * ROWS], table_parts
        ) + dot3(hidden, out_parts)
        cots = split(cot)
        back = dot3(cots, out_parts, NT)
        scaled = back * gate
        grad_act = split(scaled * (1.0 - act * act))
        grad_gate = split(scaled * act * (1.0 - gate))
        for part in range(2):
            hidden_parts[part, rows, :] = hidden[part]
            cot_parts[part, rows, :] = cots[part]
            grad_parts[part, rows, :HALF] = grad_act[part]
            grad_parts[part, rows, HALF:] = grad_gate[part]

    sums = dot2(hot_t[...], (grad_parts[0], grad_parts[1]))
    for tap in range(3):
        kept = sums[ROWS * tap : ROWS * tap + KEPT, :]
        part_ref[KEPT * tap : KEPT * tap + KEPT, :] = kept[:, :HALF]
        part_ref[KEPT * (3 + tap) : KEPT * (4 + tap), :] = kept[:, HALF:]
    cot_pair = (cot_parts[0], cot_parts[1])
    part_ref[6 * KEPT : 7 * KEPT, :] = dot2(hot_t[ROWS : 2 * ROWS, :], cot_pair)[:KEPT]
    part_ref[7 * KEPT : 7 * KEPT + HALF, :] = dot3((hidden_parts[0], hidden_parts[1]), cot_pair, TN)
    part_ref[7 * KEPT + HALF :, :] = jnp.zeros((16 * PIECE - 7 * KEPT - HALF, HALF), F32)


def local_work(dilations, tokens, embed, conv, mix, bias, out_weight, cot_fwd, cot_rev, picks, swap):
    length = cot_fwd.shape[0]
    shape = lambda *dims: jax.ShapeDtypeStruct(dims, F32)
    return pl.pallas_call(
        local_kernel,
        out_shape=[
            shape(length, HALF),
            shape(length, HALF),
            shape(16 * PIECE, HALF),
            shape(ROWS, HALF),
            shape(ROWS, HALF),
            shape(ROWS, HALF),
        ],
        in_specs=[SMEM] + [VMEM] * 10,
        out_specs=[VMEM] * 6,
        scratch_shapes=[
            pltpu.VMEM((24, 2 * HALF), F32),
            pltpu.VMEM((3 * ROWS, 2 * HALF), BF16),
            pltpu.VMEM((3 * ROWS, 2 * HALF), BF16),
            pltpu.VMEM((32, 128), F32),
            pltpu.VMEM((2 * length, 3 * ROWS), BF16),
            pltpu.VMEM((3 * ROWS, 2 * length), BF16),
            pltpu.VMEM((2, 2 * length, HALF), BF16),
            pltpu.VMEM((2, 2 * length, HALF), BF16),
            pltpu.VMEM((2, 2 * length, 2 * HALF), BF16),
        ],
        compiler_params=pltpu.CompilerParams(vmem_limit_bytes=48 << 20),
        name="local_work",
    )(dilations, tokens, embed, conv, mix, bias, out_weight, cot_fwd, cot_rev, picks, swap)


def sum_kernel(part_ref, out_ref, paired, summed, arrived, sems_a, sems_b, sems_c, sems_d):
    me = lax.axis_index("seq")
    core = lax.rem(me, 2)
    chip = lax.div(me, 2)
    twin = me + 1 - 2 * core
    chips = [exclusive(chip, bits) for bits in range(8)]
    peers = [2 * other + core for other in chips]
    barrier = pltpu.get_barrier_semaphore()
    for target in [twin] + peers[1:]:
        pl.semaphore_signal(barrier, inc=1, device_id={"seq": target}, device_id_type=MESH)
    pl.semaphore_wait(barrier, 8)

    def remote(source, landing, sems, at, target):
        return pltpu.make_async_remote_copy(
            src_ref=source,
            dst_ref=landing,
            send_sem=sems.at[0, at],
            recv_sem=sems.at[1, at],
            device_id={"seq": target},
            device_id_type=MESH,
        )

    order = (7, 5, 6, 4, 2, 3, 1, 0)
    first, second, third, fourth = {}, {}, {}, {}
    for at in order:
        first[at] = remote(part_ref.at[2 * chips[at] + 1 - core], paired.at[at], sems_a, at, twin)
        first[at].start()
    for at in order:
        first[at].wait_recv()
        summed[at] = paired[at] + part_ref[2 * chips[at] + core]
        if at:
            second[at] = remote(summed.at[at], arrived.at[at], sems_b, at, peers[at])
            second[at].start()
    total = summed[0]
    for at in order[:-1]:
        second[at].wait_recv()
        total = total + arrived[at]
    mine = 2 * chip + core
    out_ref[mine] = total
    for at in order[:-1]:
        third[at] = remote(out_ref.at[mine], out_ref.at[mine], sems_c, at, peers[at])
        third[at].start()
    fourth[0] = remote(out_ref.at[mine], out_ref.at[mine], sems_d, 0, twin)
    fourth[0].start()
    for at in order[:-1]:
        landed = out_ref.at[2 * chips[at] + core]
        remote(landed, landed, sems_c, at, peers[at]).wait_recv()
        fourth[at] = remote(landed, landed, sems_d, at, twin)
        fourth[at].start()
    for at in range(8):
        landed = out_ref.at[2 * chips[at] + 1 - core]
        remote(landed, landed, sems_d, at, twin).wait_recv()
    for at in range(8):
        first[at].wait_send()
        fourth[at].wait_send()
        if at:
            second[at].wait_send()
            third[at].wait_send()


def sum_over_devices(part):
    return pl.pallas_call(
        sum_kernel,
        out_shape=jax.ShapeDtypeStruct(part.shape, F32),
        in_specs=[VMEM],
        out_specs=VMEM,
        scratch_shapes=[pltpu.VMEM((8, PIECE, HALF), F32)] * 3 + [pltpu.SemaphoreType.DMA((2, 8))] * 4,
        compiler_params=pltpu.CompilerParams(
            collective_id=1, has_side_effects=True, vmem_limit_bytes=32 << 20
        ),
        name="sum_over_devices",
    )(part)


def gradient_kernel(
    total_ref,
    table_ref,
    tanh_ref,
    sig_ref,
    embed_ref,
    conv_ref,
    mix_ref,
    out_weight_ref,
    picks_t_ref,
    swap_ref,
    grad_embed_ref,
    grad_conv_ref,
    grad_mix_ref,
    grad_bias_ref,
    grad_out_ref,
    sums,
    cot_sums,
    wide,
):
    sums[...] = jnp.zeros_like(sums)
    cot_sums[...] = jnp.zeros_like(cot_sums)
    for tap in range(3):
        sums[tap, :KEPT, :HALF] = total_ref[KEPT * tap : KEPT * tap + KEPT, :]
        sums[tap, :KEPT, HALF:] = total_ref[KEPT * (3 + tap) : KEPT * (4 + tap), :]
    cot_sums[:KEPT, :] = total_ref[6 * KEPT : 7 * KEPT, :]
    grad_out_ref[1] = total_ref[7 * KEPT : 7 * KEPT + HALF, :]
    grad_bias_ref[1:2, :] = jnp.sum(sums[1], axis=0, keepdims=True)

    table_t = split(jnp.transpose(table_ref[...]))
    swap = swap_ref[...]
    grad = cot_sums[...]
    parts = [split(sums[tap]) for tap in range(3)]
    parts.append([dot(swap, part).astype(BF16) for part in parts[1]])
    for at in range(4):
        product = dot3(table_t, parts[at])
        if at < 3:
            grad_conv_ref[1, at] = product
        else:
            grad_mix_ref[1] = product
        grad = grad + dot3(parts[at], split(conv_ref[1, at] if at < 3 else mix_ref[1]), NT)

    grads = split(grad)
    tanh, sig = tanh_ref[...], sig_ref[...]
    hidden_t = split(jnp.transpose(tanh * sig))
    grad_out_ref[0] = dot3(hidden_t, grads)
    back = dot3(grads, split(out_weight_ref[0]), NT) * sig
    act, gate = back * (1.0 - tanh * tanh), back * tanh * (1.0 - sig)
    grad_bias_ref[0:1, :HALF] = jnp.sum(act, axis=0, keepdims=True)
    grad_bias_ref[0:1, HALF:] = jnp.sum(gate, axis=0, keepdims=True)
    picks_t = picks_t_ref[...]
    wide[:, :HALF] = dot2(picks_t, split(act))
    wide[:, HALF:] = dot2(picks_t, split(gate))
    embed_grad = dot2(picks_t, grads)[4:8]
    pieces = [wide[4 * at : 4 * at + 4, :] for at in range(4)]
    embed = split(embed_ref[...])
    for at in range(4):
        piece = split(pieces[at])
        product = dot3(embed, piece, TN)
        if at < 3:
            grad_conv_ref[0, at] = product
        else:
            grad_mix_ref[0] = product
        embed_grad = embed_grad + dot3(piece, split(conv_ref[0, at] if at < 3 else mix_ref[0]), NT)
    grad_embed_ref[...] = embed_grad


def gradients(total, table, tanh, sig, embed, conv, mix, bias, out_weight, picks_t, swap):
    return pl.pallas_call(
        gradient_kernel,
        out_shape=[
            jax.ShapeDtypeStruct(like.shape, F32) for like in (embed, conv, mix, bias, out_weight)
        ],
        in_specs=[VMEM] * 10,
        out_specs=[VMEM] * 5,
        scratch_shapes=[
            pltpu.VMEM((3, ROWS, 2 * HALF), F32),
            pltpu.VMEM((ROWS, HALF), F32),
            pltpu.VMEM((16, 2 * HALF), F32),
        ],
        compiler_params=pltpu.CompilerParams(vmem_limit_bytes=48 << 20),
        name="gradients",
    )(total, table, tanh, sig, embed, conv, mix, out_weight, picks_t, swap)


def on_device(
    tokens, dilations, embed, conv_weight, mix_weight, gate_bias, out_weight, cot_fwd, cot_rev
):
    count = lax.axis_size("seq")
    picks, picks_t, swap = [jnp.asarray(value, BF16) for value in selectors()]
    everywhere = gather_tokens(tokens.reshape(tokens.shape[0] // 128, 128), count)
    out_fwd, out_rev, part, table, tanh, sig = local_work(
        dilations, everywhere, embed, conv_weight, mix_weight, gate_bias, out_weight, cot_fwd, cot_rev, picks, swap
    )
    total = sum_over_devices(part.reshape(16, PIECE, HALF)).reshape(part.shape)
    grads = gradients(
        total, table, tanh, sig, embed, conv_weight, mix_weight, gate_bias, out_weight, picks_t, swap
    )
    return (out_fwd, out_rev, *grads)


def solution(mesh):
    in_specs = (
        P(("dp", "seq")),
        P(),
        P(),
        P(),
        P(),
        P(),
        P(),
        P(("dp", "seq"), None),
        P(("dp", "seq"), None),
    )
    out_specs = (
        P(("dp", "seq"), None),
        P(("dp", "seq"), None),
        P("dp", None),
        P("dp", None, None, None),
        P("dp", None, None),
        P("dp", None),
        P("dp", None, None),
    )
    return jax.shard_map(
        on_device, mesh=mesh, in_specs=in_specs, out_specs=out_specs, check_vma=False
    )
```

```python
import functools

import jax
import jax.numpy as jnp
import numpy as np
from jax import lax
from jax.experimental import pallas as pl
from jax.experimental.pallas import tpu as pltpu
from jax.sharding import PartitionSpec as P

MESH = pl.DeviceIdType.MESH
ROWS = 128
KEPT = 104
HALF = 256
EARLY = 24
LATE = 40
OUTSIDE = 4
NONE = 255
F32 = jnp.float32
BF16 = jnp.bfloat16
VMEM = pl.BlockSpec(memory_space=pltpu.VMEM)
HBM = pl.BlockSpec(memory_space=pltpu.HBM)


def selectors():
    row = np.arange(ROWS)
    live = row < 100
    left, own, right = row // 20, (row // 5) % 4, row % 5
    picks = np.zeros((ROWS, 16), np.float32)
    for base in range(4):
        picks[:, base] = live & (left == base)
        picks[:, 4 + base] = live & (own == base)
        picks[:, 8 + base] = live & (right == base)
        picks[:, 12 + base] = live & (own == 3 - base)
    flipped = np.array([3, 2, 1, 0, 4, 0, 0])
    other = np.where(live, flipped[right] * 20 + flipped[own] * 5 + flipped[left], row)
    swap = (other[:, None] == row).astype(np.float32)
    return picks, picks.T.copy(), swap


def split(value):
    high = value.astype(BF16)
    return high, (value - high.astype(F32)).astype(BF16)


def dot(a, b, dims=((1,), (0,))):
    return lax.dot_general(a, b, (dims, ((), ())), preferred_element_type=F32)


def dot2(exact, parts, dims=((1,), (0,))):
    return dot(exact, parts[0], dims) + dot(exact, parts[1], dims)


def dot3(a, b, dims=((1,), (0,))):
    return dot(a[0], b[0], dims) + (dot(a[0], b[1], dims) + dot(a[1], b[0], dims))


NT = ((1,), (1,))
TN = ((0,), (0,))


def sigmoid(value):
    return 0.5 * jnp.tanh(0.5 * value) + 0.5


def exclusive(value, bits):
    total = 0
    for bit in (1, 2, 4):
        digit = lax.rem(lax.div(value, bit), 2)
        total = total + bit * (1 - digit if bits & bit else digit)
    return total


def tables(embed_ref, conv_ref, mix_ref, bias_ref, out_ref, picks, swap, wide, high, low):
    wide[...] = jnp.zeros_like(wide)
    wide[16:20, :HALF] = embed_ref[...]
    embed = split(wide[16:24, :HALF])
    for at in range(4):
        weight = conv_ref[0, at] if at < 3 else mix_ref[0]
        wide[4 * at : 4 * at + 4, :] = dot3(embed, split(weight))[:4]
    mixed = dot2(picks, split(wide[:16, :])) + bias_ref[0:1, :]
    tanh = jnp.tanh(mixed[:, :HALF])
    sig = sigmoid(mixed[:, HALF:])
    wide[...] = jnp.zeros_like(wide)
    wide[4:8, :HALF] = embed_ref[...]
    table = dot2(picks, split(wide[:16, :HALF])) + dot3(split(tanh * sig), split(out_ref[0]))
    parts = split(table)
    swapped = [dot(swap, part).astype(BF16) for part in parts]
    weights = [split(conv_ref[1, at]) for at in range(3)]
    for at in range(3):
        product = dot3(parts, weights[at])
        if at == 1:
            product = product + dot3(swapped, split(mix_ref[1])) + bias_ref[1:2, :]
        high[ROWS * at : ROWS * at + ROWS, :], low[ROWS * at : ROWS * at + ROWS, :] = split(product)
    return table, tanh, sig


def beside(window):
    return jnp.concatenate([window[7:15, :], window[8:16, :], window[9:17, :]], axis=1).astype(BF16)


def chosen(length, other, sources):
    row = lax.broadcasted_iota(jnp.int32, (length, 128), 0)
    column = lax.broadcasted_iota(jnp.int32, (length, 128), 1)
    return jnp.concatenate(
        [jnp.where(row == source(column), 1.0, 0.0).astype(BF16) for source in sources], axis=1
    )


def chosen_t(length, sources):
    row = lax.broadcasted_iota(jnp.int32, (128, length), 0)
    column = lax.broadcasted_iota(jnp.int32, (128, length), 1)
    return jnp.concatenate(
        [jnp.where(column == source(row), 1.0, 0.0).astype(BF16) for source in sources], axis=0
    )


def far_sources(far, strand):
    if strand == 0:
        return [lambda at: 128 + at - far, lambda at: 128 + at, lambda at: 128 + at + far]
    return [lambda at: 255 - at + far, lambda at: 255 - at, lambda at: 255 - at - far]


def turned(base):
    return jnp.where(base == OUTSIDE, float(OUTSIDE), 3.0 - base)


def main_kernel(
    tokens_hbm,
    dilations_hbm,
    embed_hbm,
    conv_hbm,
    mix_hbm,
    bias_hbm,
    out_weight_hbm,
    cot_fwd_hbm,
    cot_rev_hbm,
    picks_hbm,
    swap_hbm,
    early_ref,
    late_ref,
    result_ref,
    table_ref,
    tanh_ref,
    sig_ref,
    dilations,
    embed_ref,
    conv_ref,
    mix_ref,
    bias_ref,
    out_weight_ref,
    cot_ref,
    picks_ref,
    swap_ref,
    landed,
    window,
    wide,
    high,
    low,
    hot,
    hot_t,
    hidden_parts,
    cot_parts,
    grad_parts,
    back_ref,
    part_early,
    part_late,
    paired_early,
    paired_late,
    summed_early,
    summed_late,
    arrived_early,
    arrived_late,
    load_sems,
    token_sems,
    pair_sems,
    chip_sems,
    spread_sems,
    twin_sems,
):
    me = lax.axis_index("seq")
    count = landed.shape[0] - 2
    length = cot_fwd_hbm.shape[0]
    barrier = pltpu.get_barrier_semaphore()
    peers = [lax.rem(me + step, count) for step in range(1, count)]
    for peer in peers:
        pl.semaphore_signal(barrier, inc=1, device_id={"seq": peer}, device_id_type=MESH)

    moves = [
        (embed_hbm, embed_ref),
        (conv_hbm, conv_ref),
        (mix_hbm, mix_ref),
        (bias_hbm, bias_ref),
        (out_weight_hbm, out_weight_ref),
        (picks_hbm, picks_ref),
        (swap_hbm, swap_ref),
        (cot_fwd_hbm, cot_ref.at[pl.ds(0, length)]),
        (cot_rev_hbm, cot_ref.at[pl.ds(length, length)]),
        (dilations_hbm, dilations),
        (tokens_hbm, landed.at[me + 1]),
    ]
    loads = []
    for at, (source, landing) in enumerate(moves):
        loads.append(pltpu.make_async_copy(source, landing, load_sems.at[at]))
        loads[-1].start()
    edge = jnp.full(landed.shape[1:], OUTSIDE, jnp.int32)
    landed[0] = edge
    landed[count + 1] = edge
    window[...] = jnp.zeros_like(window)
    part_early[...] = jnp.zeros_like(part_early)
    part_late[...] = jnp.zeros_like(part_late)

    def remote(source, landing, sems, at, target):
        return pltpu.make_async_remote_copy(
            src_ref=source,
            dst_ref=landing,
            send_sem=sems.at[0, at],
            recv_sem=sems.at[1, at],
            device_id={"seq": target},
            device_id_type=MESH,
        )

    pl.semaphore_wait(barrier, count - 1)
    token_copies = []
    for step, peer in enumerate(peers):
        token_copies.append(remote(tokens_hbm, landed.at[me + 1], token_sems, step, peer))
        token_copies[-1].start()

    for load in loads:
        load.wait()
    near, far = dilations[0], dilations[1]
    table, tanh, sig = tables(
        embed_ref, conv_ref, mix_ref, bias_ref, out_weight_ref, picks_ref[...], swap_ref[...], wide, high, low
    )
    table_ref[...], tanh_ref[...], sig_ref[...] = table, tanh, sig
    table_parts = split(table)
    out_parts = split(out_weight_ref[1])
    for block in range(4):
        rows = pl.ds(256 * block, 256)
        cots = split(cot_ref[rows, :])
        cot_parts[0, rows, :], cot_parts[1, rows, :] = cots
        back_ref[rows, :] = dot3(cots, out_parts, NT)

    for copy in token_copies:
        copy.wait_recv()
    near_move = chosen(384, 256, [lambda at: 128 + at - near, lambda at: 128 + at + near])
    lane = lax.broadcasted_iota(jnp.int32, (128, 128), 1).astype(F32)
    sub = lax.broadcasted_iota(jnp.int32, (128, 128), 0).astype(F32)
    for strand in range(2):
        block = me if strand == 0 else count - 1 - me
        window[0, 8:10, :] = landed[block][2:4].astype(F32)
        window[0, 10:14, :] = landed[block + 1].astype(F32)
        window[0, 14:16, :] = landed[block + 2][0:2].astype(F32)
        own = window[0, 8:16, :]
        moved = dot(beside(window.at[0]), near_move)
        lower, upper = moved[:, :128], moved[:, 128:]
        if strand == 0:
            code = lower * 20.0 + own * 5.0 + upper
        else:
            code = turned(upper) * 20.0 + (3.0 - own) * 5.0 + turned(lower)
        window[1, 8:16, :] = jnp.where(own == OUTSIDE, float(NONE), code)
        codes = beside(window.at[1])
        sources = far_sources(far, strand)
        across = dot(codes, chosen(384, 384, sources))
        down = dot(chosen_t(384, sources), codes, NT)
        for tap in range(3):
            taps = slice(128 * tap, 128 * tap + 128)
            for row in range(4):
                at = row + 2 if strand == 0 else 5 - row
                places = slice(512 * strand + 128 * row, 512 * strand + 128 * row + 128)
                hot[places, taps] = jnp.where(down[taps, at : at + 1] == lane, 1.0, 0.0).astype(BF16)
                hot_t[taps, places] = jnp.where(across[at : at + 1, taps] == sub, 1.0, 0.0).astype(BF16)

    for block in range(4):
        rows = pl.ds(256 * block, 256)
        mixed = dot2(hot[rows, :], (high[...], low[...]))
        act, gate = jnp.tanh(mixed[:, :HALF]), sigmoid(mixed[:, HALF:])
        hidden = split(act * gate)
        scaled = back_ref[rows, :] * gate
        grad_act = split(scaled * (1.0 - act * act))
        grad_gate = split(scaled * act * (1.0 - gate))
        for part in range(2):
            hidden_parts[part, rows, :] = hidden[part]
            grad_parts[part, rows, :HALF] = grad_act[part]
            grad_parts[part, rows, HALF:] = grad_gate[part]

    core = lax.rem(me, 2)
    chip = lax.div(me, 2)
    twin = me + 1 - 2 * core
    chips = [exclusive(chip, bits) for bits in range(8)]
    partners = [2 * other + core for other in chips]
    order = (7, 5, 6, 4, 2, 3, 1, 0)
    stages = (
        (EARLY, part_early, paired_early, summed_early, arrived_early, early_ref),
        (LATE, part_late, paired_late, summed_late, arrived_late, late_ref),
    )
    first, second, third, fourth = {}, {}, {}, {}

    def rows_of(stage, device):
        size = stages[stage][0]
        return pl.ds(pl.multiple_of(device * size, 8), size)

    def pair(stage):
        _, part, paired, _, _, _ = stages[stage]
        for at in order:
            source = part.at[rows_of(stage, 2 * chips[at] + 1 - core)]
            first[stage, at] = remote(source, paired.at[at], pair_sems, 8 * stage + at, twin)
            first[stage, at].start()

    def scatter(stage):
        _, part, paired, summed, arrived, _ = stages[stage]
        for at in order:
            first[stage, at].wait_recv()
            summed[at] = paired[at] + part[rows_of(stage, partners[at]), :]
            if at:
                second[stage, at] = remote(
                    summed.at[at], arrived.at[at], chip_sems, 8 * stage + at, partners[at]
                )
                second[stage, at].start()

    def spread(stage):
        _, _, _, summed, arrived, out = stages[stage]
        total = summed[0]
        for at in order[:-1]:
            second[stage, at].wait_recv()
            total = total + arrived[at]
        out[rows_of(stage, me), :] = total
        mine = out.at[rows_of(stage, me)]
        for at in order[:-1]:
            third[stage, at] = remote(mine, mine, spread_sems, 8 * stage + at, partners[at])
            third[stage, at].start()
        fourth[stage, 0] = remote(mine, mine, twin_sems, 8 * stage, twin)
        fourth[stage, 0].start()

    def forward(stage):
        out = stages[stage][5]
        for at in order[:-1]:
            landing = out.at[rows_of(stage, partners[at])]
            remote(landing, landing, spread_sems, 8 * stage + at, partners[at]).wait_recv()
            fourth[stage, at] = remote(landing, landing, twin_sems, 8 * stage + at, twin)
            fourth[stage, at].start()

    def finish(stage):
        out = stages[stage][5]
        for at in range(8):
            landing = out.at[rows_of(stage, 2 * chips[at] + 1 - core)]
            remote(landing, landing, twin_sems, 8 * stage + at, twin).wait_recv()
        for at in range(8):
            first[stage, at].wait_send()
            fourth[stage, at].wait_send()
            if at:
                second[stage, at].wait_send()
                third[stage, at].wait_send()

    cot_pair = (cot_parts[0], cot_parts[1])
    part_early[:HALF, :] = dot3((hidden_parts[0], hidden_parts[1]), cot_pair, TN)
    part_early[HALF : HALF + KEPT, :] = dot2(hot_t[ROWS : 2 * ROWS, :], cot_pair)[:KEPT]
    pair(0)
    sums = dot2(hot_t[...], (grad_parts[0], grad_parts[1]))
    for tap in range(3):
        kept = sums[ROWS * tap : ROWS * tap + KEPT, :]
        part_late[KEPT * tap : KEPT * tap + KEPT, :] = kept[:, :HALF]
        part_late[KEPT * (3 + tap) : KEPT * (4 + tap), :] = kept[:, HALF:]
    pair(1)
    scatter(0)
    scatter(1)
    for block in range(4):
        rows = pl.ds(256 * block, 256)
        result_ref[rows, :] = dot2(hot[rows, ROWS : 2 * ROWS], table_parts) + dot3(
            (hidden_parts[0, rows, :], hidden_parts[1, rows, :]), out_parts
        )
    spread(0)
    spread(1)
    forward(0)
    forward(1)
    finish(0)
    finish(1)
    for copy in token_copies:
        copy.wait_send()


def main(tokens, dilations, embed, conv, mix, bias, out_weight, cot_fwd, cot_rev, picks, swap, count):
    length = cot_fwd.shape[0]
    shape = lambda *dims: jax.ShapeDtypeStruct(dims, F32)
    like = lambda array: pltpu.VMEM(array.shape, array.dtype)
    sems = pltpu.SemaphoreType.DMA
    return pl.pallas_call(
        main_kernel,
        out_shape=[
            shape(16 * EARLY, HALF),
            shape(16 * LATE, HALF),
            shape(2 * length, HALF),
            shape(ROWS, HALF),
            shape(ROWS, HALF),
            shape(ROWS, HALF),
        ],
        in_specs=[HBM] * 11,
        out_specs=[VMEM] * 6,
        scratch_shapes=[
            pltpu.SMEM(dilations.shape, jnp.int32),
            like(embed),
            like(conv),
            like(mix),
            like(bias),
            like(out_weight),
            pltpu.VMEM((2 * length, HALF), F32),
            like(picks),
            like(swap),
            pltpu.VMEM((count + 2,) + tokens.shape, jnp.int32),
            pltpu.VMEM((2, 24, 128), F32),
            pltpu.VMEM((24, 2 * HALF), F32),
            pltpu.VMEM((3 * ROWS, 2 * HALF), BF16),
            pltpu.VMEM((3 * ROWS, 2 * HALF), BF16),
            pltpu.VMEM((2 * length, 3 * ROWS), BF16),
            pltpu.VMEM((3 * ROWS, 2 * length), BF16),
            pltpu.VMEM((2, 2 * length, HALF), BF16),
            pltpu.VMEM((2, 2 * length, HALF), BF16),
            pltpu.VMEM((2, 2 * length, 2 * HALF), BF16),
            pltpu.VMEM((2 * length, HALF), F32),
            pltpu.VMEM((16 * EARLY, HALF), F32),
            pltpu.VMEM((16 * LATE, HALF), F32),
        ]
        + [pltpu.VMEM((8, size, HALF), F32) for _ in range(3) for size in (EARLY, LATE)]
        + [
            sems((11,)),
            sems((2, count - 1)),
            sems((2, 16)),
            sems((2, 16)),
            sems((2, 16)),
            sems((2, 16)),
        ],
        compiler_params=pltpu.CompilerParams(
            collective_id=0, has_side_effects=True, vmem_limit_bytes=40 << 20
        ),
        name="local_work_and_sums",
    )(
        *[
            pltpu.with_memory_space_constraint(array, pltpu.HBM)
            for array in (
                tokens, dilations, embed, conv, mix, bias, out_weight, cot_fwd, cot_rev, picks, swap
            )
        ]
    )


def gradient_kernel(
    early_ref,
    late_ref,
    result_ref,
    table_ref,
    tanh_ref,
    sig_ref,
    embed_ref,
    conv_ref,
    mix_ref,
    out_weight_ref,
    picks_t_ref,
    swap_ref,
    out_fwd_hbm,
    out_rev_hbm,
    grad_embed_hbm,
    grad_conv_hbm,
    grad_mix_hbm,
    grad_bias_hbm,
    grad_out_hbm,
    grad_embed_ref,
    grad_conv_ref,
    grad_mix_ref,
    grad_bias_ref,
    grad_out_ref,
    sums,
    cot_sums,
    wide,
    sems,
):
    length = out_fwd_hbm.shape[0]
    stores = []

    def store(source, landing):
        stores.append(pltpu.make_async_copy(source, landing, sems.at[len(stores)]))
        stores[-1].start()

    store(result_ref.at[pl.ds(0, length)], out_fwd_hbm)
    store(result_ref.at[pl.ds(length, length)], out_rev_hbm)
    store(early_ref.at[pl.ds(0, HALF)], grad_out_hbm.at[1])
    sums[...] = jnp.zeros_like(sums)
    cot_sums[...] = jnp.zeros_like(cot_sums)
    for tap in range(3):
        sums[tap, :KEPT, :HALF] = late_ref[KEPT * tap : KEPT * tap + KEPT, :]
        sums[tap, :KEPT, HALF:] = late_ref[KEPT * (3 + tap) : KEPT * (4 + tap), :]
    cot_sums[:KEPT, :] = early_ref[HALF : HALF + KEPT, :]
    grad_bias_ref[1:2, :] = jnp.sum(sums[1], axis=0, keepdims=True)

    table_t = split(jnp.transpose(table_ref[...]))
    swap = swap_ref[...]
    grad = cot_sums[...]
    parts = [split(sums[tap]) for tap in range(3)]
    parts.append([dot(swap, part).astype(BF16) for part in parts[1]])
    for at in range(4):
        product = dot3(table_t, parts[at])
        if at < 3:
            grad_conv_ref[1, at] = product
            store(grad_conv_ref.at[1, at], grad_conv_hbm.at[1, at])
        else:
            grad_mix_ref[1] = product
            store(grad_mix_ref.at[1], grad_mix_hbm.at[1])
        grad = grad + dot3(parts[at], split(conv_ref[1, at] if at < 3 else mix_ref[1]), NT)

    grads = split(grad)
    tanh, sig = tanh_ref[...], sig_ref[...]
    back = dot3(grads, split(out_weight_ref[0]), NT) * sig
    act, gate = back * (1.0 - tanh * tanh), back * tanh * (1.0 - sig)
    grad_bias_ref[0:1, :HALF] = jnp.sum(act, axis=0, keepdims=True)
    grad_bias_ref[0:1, HALF:] = jnp.sum(gate, axis=0, keepdims=True)
    store(grad_bias_ref, grad_bias_hbm)
    picks_t = picks_t_ref[...]
    wide[:, :HALF] = dot2(picks_t, split(act))
    wide[:, HALF:] = dot2(picks_t, split(gate))
    pieces = [split(wide[4 * at : 4 * at + 4, :]) for at in range(4)]
    embed = split(embed_ref[...])
    for at in range(4):
        product = dot3(embed, pieces[at], TN)
        if at < 3:
            grad_conv_ref[0, at] = product
            store(grad_conv_ref.at[0, at], grad_conv_hbm.at[0, at])
        else:
            grad_mix_ref[0] = product
            store(grad_mix_ref.at[0], grad_mix_hbm.at[0])
    hidden_t = split(jnp.transpose(tanh * sig))
    grad_out_ref[0] = dot3(hidden_t, grads)
    store(grad_out_ref.at[0], grad_out_hbm.at[0])
    embed_grad = dot2(picks_t, grads)[4:8]
    for at in range(4):
        embed_grad = embed_grad + dot3(pieces[at], split(conv_ref[0, at] if at < 3 else mix_ref[0]), NT)
    grad_embed_ref[...] = embed_grad
    store(grad_embed_ref, grad_embed_hbm)
    for copy in stores:
        copy.wait()


def gradients(early, late, result, table, tanh, sig, embed, conv, mix, bias, out_weight, picks_t, swap):
    half_result = jax.ShapeDtypeStruct((result.shape[0] // 2, HALF), F32)
    likes = (embed, conv, mix, bias, out_weight)
    return pl.pallas_call(
        gradient_kernel,
        out_shape=[half_result] * 2 + [jax.ShapeDtypeStruct(like.shape, F32) for like in likes],
        in_specs=[VMEM] * 12,
        out_specs=[HBM] * 7,
        scratch_shapes=[pltpu.VMEM(like.shape, F32) for like in likes]
        + [
            pltpu.VMEM((3, ROWS, 2 * HALF), F32),
            pltpu.VMEM((ROWS, HALF), F32),
            pltpu.VMEM((16, 2 * HALF), F32),
            pltpu.SemaphoreType.DMA((14,)),
        ],
        compiler_params=pltpu.CompilerParams(vmem_limit_bytes=24 << 20),
        name="gradients",
    )(early, late, result, table, tanh, sig, embed, conv, mix, out_weight, picks_t, swap)


def on_device(
    tokens, dilations, embed, conv_weight, mix_weight, gate_bias, out_weight, cot_fwd, cot_rev
):
    count = lax.axis_size("seq")
    picks, picks_t, swap = [jnp.asarray(value, BF16) for value in selectors()]
    weights = (embed, conv_weight, mix_weight, gate_bias, out_weight)
    sums = main(
        tokens.reshape(tokens.shape[0] // 128, 128), dilations, *weights, cot_fwd, cot_rev, picks, swap, count
    )
    return tuple(gradients(*sums, *weights, picks_t, swap))


def solution(mesh):
    in_specs = (
        P(("dp", "seq")),
        P(),
        P(),
        P(),
        P(),
        P(),
        P(),
        P(("dp", "seq"), None),
        P(("dp", "seq"), None),
    )
    out_specs = (
        P(("dp", "seq"), None),
        P(("dp", "seq"), None),
        P("dp", None),
        P("dp", None, None, None),
        P("dp", None, None),
        P("dp", None),
        P("dp", None, None),
    )
    return jax.shard_map(
        on_device, mesh=mesh, in_specs=in_specs, out_specs=out_specs, check_vma=False
    )
```

```python
import functools

import jax
import jax.numpy as jnp
import numpy as np
from jax import lax
from jax.experimental import pallas as pl
from jax.experimental.pallas import tpu as pltpu
from jax.sharding import PartitionSpec as P

MESH = pl.DeviceIdType.MESH
ROWS = 128
INNER = 64
EDGE = 16
KEPT = INNER + 2 * EDGE
HALF = 256
GATE_PIECE = 56
EDGE_PIECE = 32
OUT_PIECE = 32
SENT = GATE_PIECE + EDGE_PIECE
OUTSIDE = 4
NONE = 255
F32 = jnp.float32
BF16 = jnp.bfloat16
VMEM = pl.BlockSpec(memory_space=pltpu.VMEM)
HBM = pl.BlockSpec(memory_space=pltpu.HBM)


def selectors():
    row = np.arange(ROWS)
    live = row < KEPT
    inner, before = row < INNER, row < INNER + EDGE
    low = row % 4
    own = (row // 4) % 4
    left = np.where(inner, row // 16, np.where(before, OUTSIDE, low))
    right = np.where(inner | before, low, OUTSIDE)
    picks = np.zeros((ROWS, 16), np.float32)
    for base in range(4):
        picks[:, base] = live & (left == base)
        picks[:, 4 + base] = live & (own == base)
        picks[:, 8 + base] = live & (right == base)
        picks[:, 12 + base] = live & (own == 3 - base)
    flipped = np.array([3, 2, 1, 0, OUTSIDE])
    other = code_of(flipped[right], flipped[own], flipped[left], np.where)
    swap = (np.where(live, other, row)[:, None] == row).astype(np.float32)
    return picks, picks.T.copy(), swap


def code_of(left, own, right, where):
    inner = left * 16 + own * 4 + right
    return where(
        left == OUTSIDE, INNER + own * 4 + right, where(right == OUTSIDE, INNER + EDGE + own * 4 + left, inner)
    )


def split(value):
    high = value.astype(BF16)
    return high, (value - high.astype(F32)).astype(BF16)


def dot(a, b, dims=((1,), (0,))):
    return lax.dot_general(a, b, (dims, ((), ())), preferred_element_type=F32)


def dot2(exact, parts, dims=((1,), (0,))):
    return dot(exact, parts[0], dims) + dot(exact, parts[1], dims)


def dot3(a, b, dims=((1,), (0,))):
    return dot(a[0], b[0], dims) + (dot(a[0], b[1], dims) + dot(a[1], b[0], dims))


NT = ((1,), (1,))
TN = ((0,), (0,))


def sigmoid(value):
    return 0.5 * jnp.tanh(0.5 * value) + 0.5


def exclusive(value, bits):
    total = 0
    for bit in (1, 2, 4):
        digit = lax.rem(lax.div(value, bit), 2)
        total = total + bit * (1 - digit if bits & bit else digit)
    return total


def tables(embed_ref, conv_ref, mix_ref, bias_ref, out_ref, picks, swap, wide, high, low):
    wide[...] = jnp.zeros_like(wide)
    wide[16:20, :HALF] = embed_ref[...]
    embed = split(wide[16:24, :HALF])
    for at in range(4):
        weight = conv_ref[0, at] if at < 3 else mix_ref[0]
        wide[4 * at : 4 * at + 4, :] = dot3(embed, split(weight))[:4]
    mixed = dot2(picks, split(wide[:16, :])) + bias_ref[0:1, :]
    tanh = jnp.tanh(mixed[:, :HALF])
    sig = sigmoid(mixed[:, HALF:])
    wide[...] = jnp.zeros_like(wide)
    wide[4:8, :HALF] = embed_ref[...]
    table = dot2(picks, split(wide[:16, :HALF])) + dot3(split(tanh * sig), split(out_ref[0]))
    parts = split(table)
    swapped = [dot(swap, part).astype(BF16) for part in parts]
    weights = [split(conv_ref[1, at]) for at in range(3)]
    for at in range(3):
        product = dot3(parts, weights[at])
        if at == 1:
            product = product + dot3(swapped, split(mix_ref[1])) + bias_ref[1:2, :]
        high[ROWS * at : ROWS * at + ROWS, :], low[ROWS * at : ROWS * at + ROWS, :] = split(product)
    return table, tanh, sig


def beside(window):
    return jnp.concatenate([window[7:15, :], window[8:16, :], window[9:17, :]], axis=1).astype(BF16)


def chosen(length, other, sources):
    row = lax.broadcasted_iota(jnp.int32, (length, 128), 0)
    column = lax.broadcasted_iota(jnp.int32, (length, 128), 1)
    return jnp.concatenate(
        [jnp.where(row == source(column), 1.0, 0.0).astype(BF16) for source in sources], axis=1
    )


def chosen_t(length, sources):
    row = lax.broadcasted_iota(jnp.int32, (128, length), 0)
    column = lax.broadcasted_iota(jnp.int32, (128, length), 1)
    return jnp.concatenate(
        [jnp.where(column == source(row), 1.0, 0.0).astype(BF16) for source in sources], axis=0
    )


def far_sources(far, strand):
    if strand == 0:
        return [lambda at: 128 + at - far, lambda at: 128 + at, lambda at: 128 + at + far]
    return [lambda at: 255 - at + far, lambda at: 255 - at, lambda at: 255 - at - far]


def turned(base):
    return jnp.where(base == OUTSIDE, float(OUTSIDE), 3.0 - base)


def main_kernel(
    tokens_hbm,
    dilations_hbm,
    embed_hbm,
    conv_hbm,
    mix_hbm,
    bias_hbm,
    out_weight_hbm,
    cot_fwd_hbm,
    cot_rev_hbm,
    picks_hbm,
    swap_hbm,
    gate_ref,
    out_ref,
    result_ref,
    table_t_ref,
    hidden_t_ref,
    tanh_ref,
    sig_ref,
    dilations,
    embed_ref,
    conv_ref,
    mix_ref,
    bias_ref,
    out_weight_ref,
    cot_ref,
    picks_ref,
    swap_ref,
    landed,
    window,
    wide,
    high,
    low,
    hot,
    hot_t,
    hidden_parts,
    cot_parts,
    grad_parts,
    back_ref,
    part_gate,
    part_out,
    part_edge,
    paired_gate,
    paired_out,
    summed_gate,
    summed_out,
    arrived_gate,
    arrived_out,
    load_sems,
    token_sems,
    pair_sems,
    chip_sems,
    spread_sems,
    twin_sems,
    edge_sems,
):
    me = lax.axis_index("seq")
    count = landed.shape[0] - 2
    length = cot_fwd_hbm.shape[0]
    barrier = pltpu.get_barrier_semaphore()
    peers = [lax.rem(me + step, count) for step in range(1, count)]
    for peer in peers:
        pl.semaphore_signal(barrier, inc=1, device_id={"seq": peer}, device_id_type=MESH)

    moves = [
        (embed_hbm, embed_ref),
        (conv_hbm, conv_ref),
        (mix_hbm, mix_ref),
        (bias_hbm, bias_ref),
        (out_weight_hbm, out_weight_ref),
        (picks_hbm, picks_ref),
        (swap_hbm, swap_ref),
        (cot_fwd_hbm, cot_ref.at[pl.ds(0, length)]),
        (cot_rev_hbm, cot_ref.at[pl.ds(length, length)]),
        (dilations_hbm, dilations),
        (tokens_hbm, landed.at[me + 1]),
    ]
    loads = []
    for at, (source, landing) in enumerate(moves):
        loads.append(pltpu.make_async_copy(source, landing, load_sems.at[at]))
        loads[-1].start()
    edge = jnp.full(landed.shape[1:], OUTSIDE, jnp.int32)
    landed[0] = edge
    landed[count + 1] = edge
    window[...] = jnp.zeros_like(window)
    part_edge[...] = jnp.zeros_like(part_edge)

    def remote(source, landing, sems, at, target):
        return pltpu.make_async_remote_copy(
            src_ref=source,
            dst_ref=landing,
            send_sem=sems.at[0, at],
            recv_sem=sems.at[1, at],
            device_id={"seq": target},
            device_id_type=MESH,
        )

    pl.semaphore_wait(barrier, count - 1)
    token_copies = []
    for step, peer in enumerate(peers):
        token_copies.append(remote(tokens_hbm, landed.at[me + 1], token_sems, step, peer))
        token_copies[-1].start()

    for load in loads:
        load.wait()
    near, far = dilations[0], dilations[1]
    table, tanh, sig = tables(
        embed_ref, conv_ref, mix_ref, bias_ref, out_weight_ref, picks_ref[...], swap_ref[...], wide, high, low
    )
    tanh_ref[...], sig_ref[...] = tanh, sig
    table_parts = split(table)
    for ref, value in ((table_t_ref, table), (hidden_t_ref, tanh * sig)):
        upper, lower = split(jnp.transpose(value))
        ref[:, :ROWS], ref[:, ROWS : 2 * ROWS], ref[:, 2 * ROWS :] = upper, upper, lower
    out_parts = split(out_weight_ref[1])
    for block in range(4):
        rows = pl.ds(256 * block, 256)
        cots = split(cot_ref[rows, :])
        cot_parts[0, rows, :], cot_parts[1, rows, :] = cots
        back_ref[rows, :] = dot3(cots, out_parts, NT)

    for copy in token_copies:
        copy.wait_recv()
    near_move = chosen(384, 256, [lambda at: 128 + at - near, lambda at: 128 + at + near])
    lane = lax.broadcasted_iota(jnp.int32, (128, 128), 1).astype(F32)
    sub = lax.broadcasted_iota(jnp.int32, (128, 128), 0).astype(F32)
    for strand in range(2):
        block = me if strand == 0 else count - 1 - me
        window[0, 8:10, :] = landed[block][2:4].astype(F32)
        window[0, 10:14, :] = landed[block + 1].astype(F32)
        window[0, 14:16, :] = landed[block + 2][0:2].astype(F32)
        own = window[0, 8:16, :]
        moved = dot(beside(window.at[0]), near_move)
        lower, upper = moved[:, :128], moved[:, 128:]
        if strand == 0:
            code = code_of(lower, own, upper, jnp.where)
        else:
            code = code_of(turned(upper), 3.0 - own, turned(lower), jnp.where)
        window[1, 8:16, :] = jnp.where(own == OUTSIDE, float(NONE), code)
        codes = beside(window.at[1])
        sources = far_sources(far, strand)
        across = dot(codes, chosen(384, 384, sources))
        down = dot(chosen_t(384, sources), codes, NT)
        for tap in range(3):
            taps = slice(128 * tap, 128 * tap + 128)
            for row in range(4):
                at = row + 2 if strand == 0 else 5 - row
                places = slice(512 * strand + 128 * row, 512 * strand + 128 * row + 128)
                hot[places, taps] = jnp.where(down[taps, at : at + 1] == lane, 1.0, 0.0).astype(BF16)
                hot_t[KEPT * tap : KEPT * tap + KEPT, places] = jnp.where(
                    across[at : at + 1, taps] == sub[:KEPT], 1.0, 0.0
                ).astype(BF16)

    for block in range(4):
        rows = pl.ds(256 * block, 256)
        mixed = dot2(hot[rows, :], (high[...], low[...]))
        act, gate = jnp.tanh(mixed[:, :HALF]), sigmoid(mixed[:, HALF:])
        hidden = split(act * gate)
        scaled = back_ref[rows, :] * gate
        grad_act = split(scaled * (1.0 - act * act))
        grad_gate = split(scaled * act * (1.0 - gate))
        for part in range(2):
            hidden_parts[part, rows, :] = hidden[part]
            grad_parts[part, rows, :HALF] = grad_act[part]
            grad_parts[part, rows, HALF:] = grad_gate[part]

    core = lax.rem(me, 2)
    chip = lax.div(me, 2)
    twin = me + 1 - 2 * core
    chips = [exclusive(chip, bits) for bits in range(8)]
    partners = [2 * other + core for other in chips]
    order = (7, 5, 6, 4, 2, 3, 1, 0)
    stages = (
        (GATE_PIECE, SENT, part_gate, paired_gate, summed_gate, arrived_gate, gate_ref),
        (OUT_PIECE, OUT_PIECE, part_out, paired_out, summed_out, arrived_out, out_ref),
    )
    first, second, third, fourth, edges = {}, {}, {}, {}, {}
    source_chip = 7 * core
    is_source = chip == source_chip

    def rows_of(size, device):
        return pl.ds(pl.multiple_of(device * size, 8), size)

    def landing_of(stage, device):
        return stages[stage][6].at[rows_of(stages[stage][1], device)]

    def edge_landing(device):
        return gate_ref.at[pl.ds(pl.multiple_of(device * SENT + GATE_PIECE, 8), EDGE_PIECE)]

    def edge_copy(at):
        return pltpu.make_async_remote_copy(
            src_ref=part_edge.at[rows_of(EDGE_PIECE, chips[at])],
            dst_ref=edge_landing(partners[at]),
            send_sem=edge_sems.at[at],
            recv_sem=edge_sems.at[0],
            device_id={"seq": partners[at]},
            device_id_type=MESH,
        )

    def pair(stage):
        size, _, part, paired, _, _, _ = stages[stage]
        for at in order:
            source = part.at[rows_of(size, 2 * chips[at] + 1 - core)]
            first[stage, at] = remote(source, paired.at[at], pair_sems, 8 * stage + at, twin)
            first[stage, at].start()

    def scatter(stage):
        size, _, part, paired, summed, arrived, _ = stages[stage]
        for at in order:
            first[stage, at].wait_recv()
            summed[at] = paired[at] + part[rows_of(size, partners[at]), :]
            if at:
                second[stage, at] = remote(
                    summed.at[at], arrived.at[at], chip_sems, 8 * stage + at, partners[at]
                )
                second[stage, at].start()

    def spread(stage):
        size, sent, _, _, summed, arrived, out = stages[stage]
        total = summed[0]
        for at in order[:-1]:
            second[stage, at].wait_recv()
            total = total + arrived[at]
        out[pl.ds(pl.multiple_of(me * sent, 8), size), :] = total
        mine = landing_of(stage, me)
        for at in order[:-1]:
            third[stage, at] = remote(mine, mine, spread_sems, 8 * stage + at, partners[at])
            third[stage, at].start()
        fourth[stage, 0] = remote(mine, mine, twin_sems, 8 * stage, twin)
        fourth[stage, 0].start()

    def forward(stage):
        for at in order[:-1]:
            landing = landing_of(stage, partners[at])
            remote(landing, landing, spread_sems, 8 * stage + at, partners[at]).wait_recv()
            fourth[stage, at] = remote(landing, landing, twin_sems, 8 * stage + at, twin)
            fourth[stage, at].start()

    def finish(stage):
        for at in range(8):
            landing = landing_of(stage, 2 * chips[at] + 1 - core)
            remote(landing, landing, twin_sems, 8 * stage + at, twin).wait_recv()
        for at in range(8):
            first[stage, at].wait_send()
            fourth[stage, at].wait_send()
            if at:
                second[stage, at].wait_send()
                third[stage, at].wait_send()

    cot_pair = (cot_parts[0], cot_parts[1])
    sums = dot2(hot_t[...], (grad_parts[0], grad_parts[1]))
    cot_sums = dot2(hot_t[KEPT : 2 * KEPT, :], cot_pair)
    columns = [
        sums[KEPT * tap : KEPT * tap + KEPT, 128 * at : 128 * at + 128] for tap in range(3) for at in range(4)
    ] + [cot_sums[:, :128], cot_sums[:, 128:]]
    for at, column in enumerate(columns):
        part_gate[INNER * at : INNER * at + INNER, :] = column[:INNER]
    pair(0)
    for at, column in enumerate(columns):
        part_edge[EDGE * at : EDGE * at + EDGE, :] = jnp.where(
            me == 0, column[INNER : INNER + EDGE], column[INNER + EDGE :]
        )

    @pl.when(is_source)
    def _():
        for at in order[:-1]:
            edge_copy(at).start()
        own_rows = pl.ds(pl.multiple_of(me * SENT + GATE_PIECE, 8), EDGE_PIECE)
        gate_ref[own_rows, :] = part_edge[rows_of(EDGE_PIECE, chip), :]

    product = dot3((hidden_parts[0], hidden_parts[1]), cot_pair, TN)
    part_out[:HALF, :], part_out[HALF:, :] = product[:, :128], product[:, 128:]
    scatter(0)
    pair(1)
    scatter(1)
    for block in range(4):
        rows = pl.ds(256 * block, 256)
        result_ref[rows, :] = dot2(hot[rows, ROWS : 2 * ROWS], table_parts) + dot3(
            (hidden_parts[0, rows, :], hidden_parts[1, rows, :]), out_parts
        )

    @pl.when(jnp.logical_not(is_source))
    def _():
        edge_copy(0).wait_recv()

    spread(0)
    spread(1)
    forward(0)
    forward(1)
    finish(0)
    finish(1)
    for copy in token_copies:
        copy.wait_send()

    @pl.when(is_source)
    def _():
        for at in order[:-1]:
            edge_copy(at).wait_send()


def main(tokens, dilations, embed, conv, mix, bias, out_weight, cot_fwd, cot_rev, picks, swap, count):
    length = cot_fwd.shape[0]
    shape = lambda *dims: jax.ShapeDtypeStruct(dims, F32)
    like = lambda array: pltpu.VMEM(array.shape, array.dtype)
    sems = pltpu.SemaphoreType.DMA
    return pl.pallas_call(
        main_kernel,
        out_shape=[
            shape(count * SENT, 128),
            shape(count * OUT_PIECE, 128),
            shape(2 * length, HALF),
            jax.ShapeDtypeStruct((HALF, 3 * ROWS), BF16),
            jax.ShapeDtypeStruct((HALF, 3 * ROWS), BF16),
            shape(ROWS, HALF),
            shape(ROWS, HALF),
        ],
        in_specs=[HBM] * 11,
        out_specs=[VMEM] * 7,
        scratch_shapes=[
            pltpu.SMEM(dilations.shape, jnp.int32),
            like(embed),
            like(conv),
            like(mix),
            like(bias),
            like(out_weight),
            pltpu.VMEM((2 * length, HALF), F32),
            like(picks),
            like(swap),
            pltpu.VMEM((count + 2,) + tokens.shape, jnp.int32),
            pltpu.VMEM((2, 24, 128), F32),
            pltpu.VMEM((24, 2 * HALF), F32),
            pltpu.VMEM((3 * ROWS, 2 * HALF), BF16),
            pltpu.VMEM((3 * ROWS, 2 * HALF), BF16),
            pltpu.VMEM((2 * length, 3 * ROWS), BF16),
            pltpu.VMEM((3 * KEPT, 2 * length), BF16),
            pltpu.VMEM((2, 2 * length, HALF), BF16),
            pltpu.VMEM((2, 2 * length, HALF), BF16),
            pltpu.VMEM((2, 2 * length, 2 * HALF), BF16),
            pltpu.VMEM((2 * length, HALF), F32),
            pltpu.VMEM((count * GATE_PIECE, 128), F32),
            pltpu.VMEM((count * OUT_PIECE, 128), F32),
            pltpu.VMEM((8 * EDGE_PIECE, 128), F32),
        ]
        + [pltpu.VMEM((8, size, 128), F32) for _ in range(3) for size in (GATE_PIECE, OUT_PIECE)]
        + [
            sems((11,)),
            sems((2, count - 1)),
            sems((2, 16)),
            sems((2, 16)),
            sems((2, 16)),
            sems((2, 16)),
            sems((8,)),
        ],
        compiler_params=pltpu.CompilerParams(
            collective_id=0, has_side_effects=True, vmem_limit_bytes=40 << 20
        ),
        name="local_work_and_sums",
    )(
        *[
            pltpu.with_memory_space_constraint(array, pltpu.HBM)
            for array in (
                tokens, dilations, embed, conv, mix, bias, out_weight, cot_fwd, cot_rev, picks, swap
            )
        ]
    )


def pieces_of(begin, rows, piece, place):
    at = begin
    while at < begin + rows:
        device, inside = at // piece, at % piece
        length = min(piece - inside, begin + rows - at)
        yield at - begin, place(device) + inside, length
        at += length


def gradient_kernel(
    gate_ref,
    out_ref,
    result_ref,
    table_t_ref,
    hidden_t_ref,
    tanh_ref,
    sig_ref,
    embed_ref,
    conv_ref,
    mix_ref,
    out_weight_ref,
    picks_t_ref,
    swap_ref,
    out_fwd_hbm,
    out_rev_hbm,
    grad_embed_hbm,
    grad_conv_hbm,
    grad_mix_hbm,
    grad_bias_hbm,
    grad_out_hbm,
    grad_embed_ref,
    grad_conv_ref,
    grad_mix_ref,
    grad_bias_ref,
    grad_out_ref,
    sums,
    wide,
    rows_left,
    rows_right,
    sems,
):
    length = out_fwd_hbm.shape[0]
    stores = []

    def store(source, landing):
        stores.append(pltpu.make_async_copy(source, landing, sems.at[len(stores)]))
        stores[-1].start()

    store(result_ref.at[pl.ds(0, length)], out_fwd_hbm)
    store(result_ref.at[pl.ds(length, length)], out_rev_hbm)
    for at in range(2):
        store(out_ref.at[pl.ds(HALF * at, HALF)], grad_out_hbm.at[1, :, pl.ds(128 * at, 128)])
    sums[:, KEPT:, :] = jnp.zeros((4, ROWS - KEPT, 2 * HALF), F32)
    for at in range(14):
        tap, columns = at // 4, pl.ds(128 * (at % 4), 128)
        runs = list(pieces_of(INNER * at, INNER, GATE_PIECE, lambda device: SENT * device))
        for side in range(2):
            for offset, address, size in pieces_of(
                EDGE * at, EDGE, EDGE_PIECE, lambda chip: SENT * (2 * chip + side) + GATE_PIECE
            ):
                runs.append((INNER + EDGE * side + offset, address, size))
        for offset, address, size in runs:
            sums[tap, pl.ds(offset, size), columns] = gate_ref[pl.ds(address, size), :]
    grad_bias_ref[1:2, :] = jnp.sum(sums[1], axis=0, keepdims=True)

    swap = swap_ref[...]
    grad = sums[3, :, :HALF]
    parts = [split(sums[tap]) for tap in range(3)]
    parts.append([dot(swap, part).astype(BF16) for part in parts[1]])
    table_t = table_t_ref[...]
    for at in range(4):
        upper, lower = parts[at]
        product = dot(table_t, jnp.concatenate([upper, lower, upper], axis=0))
        if at < 3:
            grad_conv_ref[1, at] = product
            store(grad_conv_ref.at[1, at], grad_conv_hbm.at[1, at])
        else:
            grad_mix_ref[1] = product
            store(grad_mix_ref.at[1], grad_mix_hbm.at[1])
        grad = grad + dot3(parts[at], split(conv_ref[1, at] if at < 3 else mix_ref[1]), NT)

    grads = split(grad)
    tanh, sig = tanh_ref[...], sig_ref[...]
    back = dot3(grads, split(out_weight_ref[0]), NT) * sig
    act, gate = back * (1.0 - tanh * tanh), back * tanh * (1.0 - sig)
    picks_t = picks_t_ref[...]
    wide[:, :HALF] = dot2(picks_t, split(act))
    wide[:, HALF:] = dot2(picks_t, split(gate))
    bases = split(embed_ref[...])
    rows_left[...] = jnp.zeros_like(rows_left)
    rows_right[...] = jnp.zeros_like(rows_right)
    pieces = [split(wide[4 * at : 4 * at + 4, :]) for at in range(4)]
    for at, part in enumerate((0, 0, 1)):
        rows_left[4 * at : 4 * at + 4, :] = bases[part].astype(F32)
    for at, part in enumerate((0, 1, 0)):
        for tap in range(4):
            rows_right[4 * at : 4 * at + 4, 512 * tap : 512 * tap + 512] = pieces[tap][part].astype(F32)
    left = rows_left[...].astype(BF16)
    for at in range(4):
        product = dot(left, rows_right[:, 512 * at : 512 * at + 512].astype(BF16), TN)
        if at < 3:
            grad_conv_ref[0, at] = product
            store(grad_conv_ref.at[0, at], grad_conv_hbm.at[0, at])
        else:
            grad_mix_ref[0] = product
            store(grad_mix_ref.at[0], grad_mix_hbm.at[0])
    grad_out_ref[...] = dot(hidden_t_ref[...], jnp.concatenate([grads[0], grads[1], grads[0]], axis=0))
    store(grad_out_ref, grad_out_hbm.at[0])
    grad_bias_ref[0:1, :HALF] = jnp.sum(act, axis=0, keepdims=True)
    grad_bias_ref[0:1, HALF:] = jnp.sum(gate, axis=0, keepdims=True)
    store(grad_bias_ref, grad_bias_hbm)
    embed_grad = dot2(picks_t, grads)[4:8]
    for at in range(4):
        embed_grad = embed_grad + dot3(pieces[at], split(conv_ref[0, at] if at < 3 else mix_ref[0]), NT)
    grad_embed_ref[...] = embed_grad
    store(grad_embed_ref, grad_embed_hbm)
    for copy in stores:
        copy.wait()


def gradients(sums, embed, conv, mix, bias, out_weight, picks_t, swap):
    half_result = jax.ShapeDtypeStruct((sums[2].shape[0] // 2, HALF), F32)
    likes = (embed, conv, mix, bias, out_weight)
    return pl.pallas_call(
        gradient_kernel,
        out_shape=[half_result] * 2 + [jax.ShapeDtypeStruct(like.shape, F32) for like in likes],
        in_specs=[VMEM] * 13,
        out_specs=[HBM] * 7,
        scratch_shapes=[pltpu.VMEM(like.shape, F32) for like in likes[:4]]
        + [
            pltpu.VMEM((HALF, HALF), F32),
            pltpu.VMEM((4, ROWS, 2 * HALF), F32),
            pltpu.VMEM((16, 2 * HALF), F32),
            pltpu.VMEM((16, HALF), F32),
            pltpu.VMEM((16, 8 * HALF), F32),
            pltpu.SemaphoreType.DMA((15,)),
        ],
        compiler_params=pltpu.CompilerParams(vmem_limit_bytes=24 << 20),
        name="gradients",
    )(*sums, embed, conv, mix, out_weight, picks_t, swap)


def on_device(
    tokens, dilations, embed, conv_weight, mix_weight, gate_bias, out_weight, cot_fwd, cot_rev
):
    count = lax.axis_size("seq")
    picks, picks_t, swap = [jnp.asarray(value, BF16) for value in selectors()]
    weights = (embed, conv_weight, mix_weight, gate_bias, out_weight)
    sums = main(
        tokens.reshape(tokens.shape[0] // 128, 128), dilations, *weights, cot_fwd, cot_rev, picks, swap, count
    )
    return tuple(gradients(sums, *weights, picks_t, swap))


def solution(mesh):
    in_specs = (
        P(("dp", "seq")),
        P(),
        P(),
        P(),
        P(),
        P(),
        P(),
        P(("dp", "seq"), None),
        P(("dp", "seq"), None),
    )
    out_specs = (
        P(("dp", "seq"), None),
        P(("dp", "seq"), None),
        P("dp", None),
        P("dp", None, None, None),
        P("dp", None, None),
        P("dp", None),
        P("dp", None, None),
    )
    return jax.shard_map(
        on_device, mesh=mesh, in_specs=in_specs, out_specs=out_specs, check_vma=False
    )
```

```python
import functools

import jax
import jax.numpy as jnp
import numpy as np
from jax import lax
from jax.experimental import pallas as pl
from jax.experimental.pallas import tpu as pltpu
from jax.sharding import PartitionSpec as P

MESH = pl.DeviceIdType.MESH
ROWS = 128
INNER = 64
EDGE = 16
KEPT = INNER + 2 * EDGE
HALF = 256
GATE_PIECE = 56
EDGE_PIECE = 32
OUT_PIECE = 32
SENT = GATE_PIECE + EDGE_PIECE
OUTSIDE = 4
NONE = 255
F32 = jnp.float32
BF16 = jnp.bfloat16
VMEM = pl.BlockSpec(memory_space=pltpu.VMEM)
HBM = pl.BlockSpec(memory_space=pltpu.HBM)


def selectors():
    row = np.arange(ROWS)
    live = row < KEPT
    inner, before = row < INNER, row < INNER + EDGE
    low = row % 4
    own = (row // 4) % 4
    left = np.where(inner, row // 16, np.where(before, OUTSIDE, low))
    right = np.where(inner | before, low, OUTSIDE)
    picks = np.zeros((ROWS, 16), np.float32)
    for base in range(4):
        picks[:, base] = live & (left == base)
        picks[:, 4 + base] = live & (own == base)
        picks[:, 8 + base] = live & (right == base)
        picks[:, 12 + base] = live & (own == 3 - base)
    flipped = np.array([3, 2, 1, 0, OUTSIDE])
    other = code_of(flipped[right], flipped[own], flipped[left], np.where)
    swap = (np.where(live, other, row)[:, None] == row).astype(np.float32)
    return picks, picks.T.copy(), swap


def code_of(left, own, right, where):
    inner = left * 16 + own * 4 + right
    return where(
        left == OUTSIDE, INNER + own * 4 + right, where(right == OUTSIDE, INNER + EDGE + own * 4 + left, inner)
    )


def split(value):
    high = value.astype(BF16)
    return high, (value - high.astype(F32)).astype(BF16)


def dot(a, b, dims=((1,), (0,))):
    return lax.dot_general(a, b, (dims, ((), ())), preferred_element_type=F32)


def dot2(exact, parts, dims=((1,), (0,))):
    return dot(exact, parts[0], dims) + dot(exact, parts[1], dims)


def dot3(a, b, dims=((1,), (0,))):
    return dot(a[0], b[0], dims) + (dot(a[0], b[1], dims) + dot(a[1], b[0], dims))


NT = ((1,), (1,))
TN = ((0,), (0,))


def sigmoid(value):
    return 0.5 * jnp.tanh(0.5 * value) + 0.5


def exclusive(value, bits):
    total = 0
    for bit in (1, 2, 4):
        digit = lax.rem(lax.div(value, bit), 2)
        total = total + bit * (1 - digit if bits & bit else digit)
    return total


def tables(embed_ref, conv_ref, mix_ref, bias_ref, out_ref, picks, swap, wide, high, low):
    wide[...] = jnp.zeros_like(wide)
    wide[16:20, :HALF] = embed_ref[...]
    embed = split(wide[16:24, :HALF])
    for at in range(4):
        weight = conv_ref[0, at] if at < 3 else mix_ref[0]
        wide[4 * at : 4 * at + 4, :] = dot3(embed, split(weight))[:4]
    mixed = dot2(picks, split(wide[:16, :])) + bias_ref[0:1, :]
    tanh = jnp.tanh(mixed[:, :HALF])
    sig = sigmoid(mixed[:, HALF:])
    wide[...] = jnp.zeros_like(wide)
    wide[4:8, :HALF] = embed_ref[...]
    table = dot2(picks, split(wide[:16, :HALF])) + dot3(split(tanh * sig), split(out_ref[0]))
    parts = split(table)
    swapped = [dot(swap, part).astype(BF16) for part in parts]
    weights = [split(conv_ref[1, at]) for at in range(3)]
    for at in range(3):
        product = dot3(parts, weights[at])
        if at == 1:
            product = product + dot3(swapped, split(mix_ref[1])) + bias_ref[1:2, :]
        high[ROWS * at : ROWS * at + ROWS, :], low[ROWS * at : ROWS * at + ROWS, :] = split(product)
    return table, tanh, sig


def beside(window):
    return jnp.concatenate([window[7:15, :], window[8:16, :], window[9:17, :]], axis=1).astype(BF16)


def chosen(length, other, sources):
    row = lax.broadcasted_iota(jnp.int32, (length, 128), 0)
    column = lax.broadcasted_iota(jnp.int32, (length, 128), 1)
    return jnp.concatenate(
        [jnp.where(row == source(column), 1.0, 0.0).astype(BF16) for source in sources], axis=1
    )


def chosen_t(length, sources):
    row = lax.broadcasted_iota(jnp.int32, (128, length), 0)
    column = lax.broadcasted_iota(jnp.int32, (128, length), 1)
    return jnp.concatenate(
        [jnp.where(column == source(row), 1.0, 0.0).astype(BF16) for source in sources], axis=0
    )


def far_sources(far, strand):
    if strand == 0:
        return [lambda at: 128 + at - far, lambda at: 128 + at, lambda at: 128 + at + far]
    return [lambda at: 255 - at + far, lambda at: 255 - at, lambda at: 255 - at - far]


def turned(base):
    return jnp.where(base == OUTSIDE, float(OUTSIDE), 3.0 - base)


def main_kernel(
    tokens_hbm,
    dilations_hbm,
    embed_hbm,
    conv_hbm,
    mix_hbm,
    bias_hbm,
    out_weight_hbm,
    cot_fwd_hbm,
    cot_rev_hbm,
    picks_hbm,
    swap_hbm,
    gate_ref,
    out_ref,
    result_ref,
    table_t_ref,
    hidden_t_ref,
    tanh_ref,
    sig_ref,
    dilations,
    embed_ref,
    conv_ref,
    mix_ref,
    bias_ref,
    out_weight_ref,
    cot_ref,
    picks_ref,
    swap_ref,
    landed,
    window,
    wide,
    high,
    low,
    hot,
    hot_t,
    hidden_parts,
    cot_parts,
    grad_parts,
    back_ref,
    part_gate,
    part_out,
    part_edge,
    paired_gate,
    paired_out,
    summed_gate,
    summed_out,
    arrived_gate,
    arrived_out,
    load_sems,
    token_sems,
    sent_sems,
    pair_sems,
    chip_sems,
    spread_sems,
    twin_sems,
    edge_sems,
):
    me = lax.axis_index("seq")
    count = landed.shape[0] - 2
    length = cot_fwd_hbm.shape[0]
    barrier = pltpu.get_barrier_semaphore()
    peers = [lax.rem(me + step, count) for step in range(1, count)]
    for peer in peers:
        pl.semaphore_signal(barrier, inc=1, device_id={"seq": peer}, device_id_type=MESH)

    moves = [
        (embed_hbm, embed_ref),
        (conv_hbm, conv_ref),
        (mix_hbm, mix_ref),
        (bias_hbm, bias_ref),
        (out_weight_hbm, out_weight_ref),
        (picks_hbm, picks_ref),
        (swap_hbm, swap_ref),
        (cot_fwd_hbm, cot_ref.at[pl.ds(0, length)]),
        (cot_rev_hbm, cot_ref.at[pl.ds(length, length)]),
        (dilations_hbm, dilations),
        (tokens_hbm, landed.at[me + 1]),
    ]
    loads = []
    for at, (source, landing) in enumerate(moves):
        loads.append(pltpu.make_async_copy(source, landing, load_sems.at[at]))
        loads[-1].start()
    edge = jnp.full(landed.shape[1:], OUTSIDE, jnp.int32)
    landed[0] = edge
    landed[count + 1] = edge
    window[...] = jnp.zeros_like(window)
    part_edge[...] = jnp.zeros_like(part_edge)

    def remote(source, landing, send_sem, recv_sem, target):
        return pltpu.make_async_remote_copy(
            src_ref=source,
            dst_ref=landing,
            send_sem=send_sem,
            recv_sem=recv_sem,
            device_id={"seq": target},
            device_id_type=MESH,
        )

    pl.semaphore_wait(barrier, count - 1)
    for peer in peers:
        remote(tokens_hbm, landed.at[me + 1], token_sems.at[0], token_sems.at[1], peer).start()
    every = landed.at[pl.ds(0, count - 1)]
    all_tokens = remote(every, every, token_sems.at[0], token_sems.at[1], peers[0])

    for load in loads:
        load.wait()
    near, far = dilations[0], dilations[1]
    table, tanh, sig = tables(
        embed_ref, conv_ref, mix_ref, bias_ref, out_weight_ref, picks_ref[...], swap_ref[...], wide, high, low
    )
    tanh_ref[...], sig_ref[...] = tanh, sig
    table_parts = split(table)
    for ref, value in ((table_t_ref, table), (hidden_t_ref, tanh * sig)):
        upper, lower = split(jnp.transpose(value))
        ref[:, :ROWS], ref[:, ROWS : 2 * ROWS], ref[:, 2 * ROWS :] = upper, upper, lower
    out_parts = split(out_weight_ref[1])
    for block in range(4):
        rows = pl.ds(256 * block, 256)
        cots = split(cot_ref[rows, :])
        cot_parts[0, rows, :], cot_parts[1, rows, :] = cots
        back_ref[rows, :] = dot3(cots, out_parts, NT)

    all_tokens.wait_recv()
    near_move = chosen(384, 256, [lambda at: 128 + at - near, lambda at: 128 + at + near])
    lane = lax.broadcasted_iota(jnp.int32, (128, 128), 1).astype(F32)
    sub = lax.broadcasted_iota(jnp.int32, (128, 128), 0).astype(F32)
    for strand in range(2):
        block = me if strand == 0 else count - 1 - me
        window[0, 8:10, :] = landed[block][2:4].astype(F32)
        window[0, 10:14, :] = landed[block + 1].astype(F32)
        window[0, 14:16, :] = landed[block + 2][0:2].astype(F32)
        own = window[0, 8:16, :]
        moved = dot(beside(window.at[0]), near_move)
        lower, upper = moved[:, :128], moved[:, 128:]
        if strand == 0:
            code = code_of(lower, own, upper, jnp.where)
        else:
            code = code_of(turned(upper), 3.0 - own, turned(lower), jnp.where)
        window[1, 8:16, :] = jnp.where(own == OUTSIDE, float(NONE), code)
        codes = beside(window.at[1])
        sources = far_sources(far, strand)
        across = dot(codes, chosen(384, 384, sources))
        down = dot(chosen_t(384, sources), codes, NT)
        for tap in range(3):
            taps = slice(128 * tap, 128 * tap + 128)
            for row in range(4):
                at = row + 2 if strand == 0 else 5 - row
                places = slice(512 * strand + 128 * row, 512 * strand + 128 * row + 128)
                hot[places, taps] = jnp.where(down[taps, at : at + 1] == lane, 1.0, 0.0).astype(BF16)
                hot_t[KEPT * tap : KEPT * tap + KEPT, places] = jnp.where(
                    across[at : at + 1, taps] == sub[:KEPT], 1.0, 0.0
                ).astype(BF16)

    for block in range(4):
        rows = pl.ds(256 * block, 256)
        mixed = dot2(hot[rows, :], (high[...], low[...]))
        act, gate = jnp.tanh(mixed[:, :HALF]), sigmoid(mixed[:, HALF:])
        hidden = split(act * gate)
        scaled = back_ref[rows, :] * gate
        grad_act = split(scaled * (1.0 - act * act))
        grad_gate = split(scaled * act * (1.0 - gate))
        for part in range(2):
            hidden_parts[part, rows, :] = hidden[part]
            grad_parts[part, rows, :HALF] = grad_act[part]
            grad_parts[part, rows, HALF:] = grad_gate[part]

    core = lax.rem(me, 2)
    chip = lax.div(me, 2)
    twin = me + 1 - 2 * core
    chips = [exclusive(chip, bits) for bits in range(8)]
    partners = [2 * other + core for other in chips]
    order = (7, 5, 6, 4, 2, 3, 1, 0)
    stages = (
        (GATE_PIECE, SENT, part_gate, paired_gate, summed_gate, arrived_gate, gate_ref),
        (OUT_PIECE, OUT_PIECE, part_out, paired_out, summed_out, arrived_out, out_ref),
    )
    first = {}
    source_chip = 7 * core
    is_source = chip == source_chip

    def rows_of(size, device):
        return pl.ds(pl.multiple_of(device * size, 8), size)

    def landing_of(stage, device):
        return stages[stage][6].at[rows_of(stages[stage][1], device)]

    def edge_landing(device):
        return gate_ref.at[pl.ds(pl.multiple_of(device * SENT + GATE_PIECE, 8), EDGE_PIECE)]

    def edge_copy(at):
        return pltpu.make_async_remote_copy(
            src_ref=part_edge.at[rows_of(EDGE_PIECE, chips[at])],
            dst_ref=edge_landing(partners[at]),
            send_sem=edge_sems.at[0],
            recv_sem=edge_sems.at[1],
            device_id={"seq": partners[at]},
            device_id_type=MESH,
        )

    def pair(stage):
        size, _, part, paired, _, _, _ = stages[stage]
        for at in order:
            source = part.at[rows_of(size, 2 * chips[at] + 1 - core)]
            first[stage, at] = remote(
                source, paired.at[at], sent_sems.at[stage], pair_sems.at[8 * stage + at], twin
            )
            first[stage, at].start()

    def scatter(stage):
        size, _, part, paired, summed, arrived, _ = stages[stage]
        for at in order:
            first[stage, at].wait_recv()
            summed[at] = paired[at] + part[rows_of(size, partners[at]), :]
            if at:
                remote(
                    summed.at[at], arrived.at[at], sent_sems.at[2 + stage], chip_sems.at[stage], partners[at]
                ).start()

    def spread(stage):
        size, sent, _, _, summed, arrived, out = stages[stage]
        whole = arrived.at[pl.ds(1, 7)]
        remote(whole, whole, sent_sems.at[2 + stage], chip_sems.at[stage], twin).wait_recv()
        total = summed[0]
        for at in order[:-1]:
            total = total + arrived[at]
        out[pl.ds(pl.multiple_of(me * sent, 8), size), :] = total
        mine = landing_of(stage, me)
        for at in order[:-1]:
            remote(
                mine, mine, sent_sems.at[4 + stage], spread_sems.at[8 * stage + at], partners[at]
            ).start()
        remote(mine, mine, sent_sems.at[6 + stage], twin_sems.at[stage], twin).start()

    def forward(stage):
        for at in order[:-1]:
            landing = landing_of(stage, partners[at])
            remote(
                landing, landing, sent_sems.at[4 + stage], spread_sems.at[8 * stage + at], partners[at]
            ).wait_recv()
            remote(landing, landing, sent_sems.at[6 + stage], twin_sems.at[stage], twin).start()

    def finish(stage):
        size, sent, part, _, _, _, out = stages[stage]
        whole = out.at[pl.ds(0, 8 * sent)]
        remote(whole, whole, sent_sems.at[6 + stage], twin_sems.at[stage], twin).wait_recv()
        for step, (ref, rows) in enumerate(((part, 8 * size), (part, 7 * size), (out, 7 * sent), (out, 8 * sent))):
            view = ref.at[pl.ds(0, rows)]
            remote(view, view, sent_sems.at[2 * step + stage], twin_sems.at[stage], twin).wait_send()

    cot_pair = (cot_parts[0], cot_parts[1])
    sums = dot2(hot_t[...], (grad_parts[0], grad_parts[1]))
    cot_sums = dot2(hot_t[KEPT : 2 * KEPT, :], cot_pair)
    columns = [
        sums[KEPT * tap : KEPT * tap + KEPT, 128 * at : 128 * at + 128] for tap in range(3) for at in range(4)
    ] + [cot_sums[:, :128], cot_sums[:, 128:]]
    for at, column in enumerate(columns):
        part_gate[INNER * at : INNER * at + INNER, :] = column[:INNER]
    pair(0)
    for at, column in enumerate(columns):
        part_edge[EDGE * at : EDGE * at + EDGE, :] = jnp.where(
            me == 0, column[INNER : INNER + EDGE], column[INNER + EDGE :]
        )

    @pl.when(is_source)
    def _():
        for at in order[:-1]:
            edge_copy(at).start()
        own_rows = pl.ds(pl.multiple_of(me * SENT + GATE_PIECE, 8), EDGE_PIECE)
        gate_ref[own_rows, :] = part_edge[rows_of(EDGE_PIECE, chip), :]

    product = dot3((hidden_parts[0], hidden_parts[1]), cot_pair, TN)
    part_out[:HALF, :], part_out[HALF:, :] = product[:, :128], product[:, 128:]
    scatter(0)
    pair(1)
    scatter(1)
    for block in range(4):
        rows = pl.ds(256 * block, 256)
        result_ref[rows, :] = dot2(hot[rows, ROWS : 2 * ROWS], table_parts) + dot3(
            (hidden_parts[0, rows, :], hidden_parts[1, rows, :]), out_parts
        )

    @pl.when(jnp.logical_not(is_source))
    def _():
        edge_copy(0).wait_recv()

    spread(0)
    spread(1)
    forward(0)
    forward(1)
    finish(0)
    finish(1)
    all_tokens.wait_send()

    @pl.when(is_source)
    def _():
        view = part_edge.at[pl.ds(0, 7 * EDGE_PIECE)]
        remote(view, view, edge_sems.at[0], edge_sems.at[1], twin).wait_send()


def main(tokens, dilations, embed, conv, mix, bias, out_weight, cot_fwd, cot_rev, picks, swap, count):
    length = cot_fwd.shape[0]
    shape = lambda *dims: jax.ShapeDtypeStruct(dims, F32)
    like = lambda array: pltpu.VMEM(array.shape, array.dtype)
    sems = pltpu.SemaphoreType.DMA
    return pl.pallas_call(
        main_kernel,
        out_shape=[
            shape(count * SENT, 128),
            shape(count * OUT_PIECE, 128),
            shape(2 * length, HALF),
            jax.ShapeDtypeStruct((HALF, 3 * ROWS), BF16),
            jax.ShapeDtypeStruct((HALF, 3 * ROWS), BF16),
            shape(ROWS, HALF),
            shape(ROWS, HALF),
        ],
        in_specs=[HBM] * 11,
        out_specs=[VMEM] * 7,
        scratch_shapes=[
            pltpu.SMEM(dilations.shape, jnp.int32),
            like(embed),
            like(conv),
            like(mix),
            like(bias),
            like(out_weight),
            pltpu.VMEM((2 * length, HALF), F32),
            like(picks),
            like(swap),
            pltpu.VMEM((count + 2,) + tokens.shape, jnp.int32),
            pltpu.VMEM((2, 24, 128), F32),
            pltpu.VMEM((24, 2 * HALF), F32),
            pltpu.VMEM((3 * ROWS, 2 * HALF), BF16),
            pltpu.VMEM((3 * ROWS, 2 * HALF), BF16),
            pltpu.VMEM((2 * length, 3 * ROWS), BF16),
            pltpu.VMEM((3 * KEPT, 2 * length), BF16),
            pltpu.VMEM((2, 2 * length, HALF), BF16),
            pltpu.VMEM((2, 2 * length, HALF), BF16),
            pltpu.VMEM((2, 2 * length, 2 * HALF), BF16),
            pltpu.VMEM((2 * length, HALF), F32),
            pltpu.VMEM((count * GATE_PIECE, 128), F32),
            pltpu.VMEM((count * OUT_PIECE, 128), F32),
            pltpu.VMEM((8 * EDGE_PIECE, 128), F32),
        ]
        + [pltpu.VMEM((8, size, 128), F32) for _ in range(3) for size in (GATE_PIECE, OUT_PIECE)]
        + [
            sems((11,)),
            sems((2,)),
            sems((8,)),
            sems((16,)),
            sems((2,)),
            sems((16,)),
            sems((2,)),
            sems((2,)),
        ],
        compiler_params=pltpu.CompilerParams(
            collective_id=0, has_side_effects=True, vmem_limit_bytes=40 << 20
        ),
        name="local_work_and_sums",
    )(
        *[
            pltpu.with_memory_space_constraint(array, pltpu.HBM)
            for array in (
                tokens, dilations, embed, conv, mix, bias, out_weight, cot_fwd, cot_rev, picks, swap
            )
        ]
    )


def pieces_of(begin, rows, piece, place):
    at = begin
    while at < begin + rows:
        device, inside = at // piece, at % piece
        length = min(piece - inside, begin + rows - at)
        yield at - begin, place(device) + inside, length
        at += length


def gradient_kernel(
    gate_ref,
    out_ref,
    result_ref,
    table_t_ref,
    hidden_t_ref,
    tanh_ref,
    sig_ref,
    embed_ref,
    conv_ref,
    mix_ref,
    out_weight_ref,
    picks_t_ref,
    swap_ref,
    out_fwd_hbm,
    out_rev_hbm,
    grad_embed_hbm,
    grad_conv_hbm,
    grad_mix_hbm,
    grad_bias_hbm,
    grad_out_hbm,
    grad_embed_ref,
    grad_conv_ref,
    grad_mix_ref,
    grad_bias_ref,
    grad_out_ref,
    sums,
    wide,
    rows_left,
    rows_right,
    sems,
):
    length = out_fwd_hbm.shape[0]
    stores = []

    def store(source, landing):
        stores.append(pltpu.make_async_copy(source, landing, sems.at[len(stores)]))
        stores[-1].start()

    store(result_ref.at[pl.ds(0, length)], out_fwd_hbm)
    store(result_ref.at[pl.ds(length, length)], out_rev_hbm)
    for at in range(2):
        store(out_ref.at[pl.ds(HALF * at, HALF)], grad_out_hbm.at[1, :, pl.ds(128 * at, 128)])
    sums[:, KEPT:, :] = jnp.zeros((4, ROWS - KEPT, 2 * HALF), F32)
    for at in range(14):
        tap, columns = at // 4, pl.ds(128 * (at % 4), 128)
        runs = list(pieces_of(INNER * at, INNER, GATE_PIECE, lambda device: SENT * device))
        for side in range(2):
            for offset, address, size in pieces_of(
                EDGE * at, EDGE, EDGE_PIECE, lambda chip: SENT * (2 * chip + side) + GATE_PIECE
            ):
                runs.append((INNER + EDGE * side + offset, address, size))
        for offset, address, size in runs:
            sums[tap, pl.ds(offset, size), columns] = gate_ref[pl.ds(address, size), :]
    grad_bias_ref[1:2, :] = jnp.sum(sums[1], axis=0, keepdims=True)

    swap = swap_ref[...]
    grad = sums[3, :, :HALF]
    parts = [split(sums[tap]) for tap in range(3)]
    parts.append([dot(swap, part).astype(BF16) for part in parts[1]])
    table_t = table_t_ref[...]
    for at in range(4):
        upper, lower = parts[at]
        product = dot(table_t, jnp.concatenate([upper, lower, upper], axis=0))
        if at < 3:
            grad_conv_ref[1, at] = product
            store(grad_conv_ref.at[1, at], grad_conv_hbm.at[1, at])
        else:
            grad_mix_ref[1] = product
            store(grad_mix_ref.at[1], grad_mix_hbm.at[1])
        grad = grad + dot3(parts[at], split(conv_ref[1, at] if at < 3 else mix_ref[1]), NT)

    grads = split(grad)
    tanh, sig = tanh_ref[...], sig_ref[...]
    back = dot3(grads, split(out_weight_ref[0]), NT) * sig
    act, gate = back * (1.0 - tanh * tanh), back * tanh * (1.0 - sig)
    picks_t = picks_t_ref[...]
    wide[:, :HALF] = dot2(picks_t, split(act))
    wide[:, HALF:] = dot2(picks_t, split(gate))
    bases = split(embed_ref[...])
    rows_left[...] = jnp.zeros_like(rows_left)
    rows_right[...] = jnp.zeros_like(rows_right)
    pieces = [split(wide[4 * at : 4 * at + 4, :]) for at in range(4)]
    for at, part in enumerate((0, 0, 1)):
        rows_left[4 * at : 4 * at + 4, :] = bases[part].astype(F32)
    for at, part in enumerate((0, 1, 0)):
        for tap in range(4):
            rows_right[4 * at : 4 * at + 4, 512 * tap : 512 * tap + 512] = pieces[tap][part].astype(F32)
    left = rows_left[...].astype(BF16)
    for at in range(4):
        product = dot(left, rows_right[:, 512 * at : 512 * at + 512].astype(BF16), TN)
        if at < 3:
            grad_conv_ref[0, at] = product
            store(grad_conv_ref.at[0, at], grad_conv_hbm.at[0, at])
        else:
            grad_mix_ref[0] = product
            store(grad_mix_ref.at[0], grad_mix_hbm.at[0])
    grad_out_ref[...] = dot(hidden_t_ref[...], jnp.concatenate([grads[0], grads[1], grads[0]], axis=0))
    store(grad_out_ref, grad_out_hbm.at[0])
    grad_bias_ref[0:1, :HALF] = jnp.sum(act, axis=0, keepdims=True)
    grad_bias_ref[0:1, HALF:] = jnp.sum(gate, axis=0, keepdims=True)
    store(grad_bias_ref, grad_bias_hbm)
    embed_grad = dot2(picks_t, grads)[4:8]
    for at in range(4):
        embed_grad = embed_grad + dot3(pieces[at], split(conv_ref[0, at] if at < 3 else mix_ref[0]), NT)
    grad_embed_ref[...] = embed_grad
    store(grad_embed_ref, grad_embed_hbm)
    for copy in stores:
        copy.wait()


def gradients(sums, embed, conv, mix, bias, out_weight, picks_t, swap):
    half_result = jax.ShapeDtypeStruct((sums[2].shape[0] // 2, HALF), F32)
    likes = (embed, conv, mix, bias, out_weight)
    return pl.pallas_call(
        gradient_kernel,
        out_shape=[half_result] * 2 + [jax.ShapeDtypeStruct(like.shape, F32) for like in likes],
        in_specs=[VMEM] * 13,
        out_specs=[HBM] * 7,
        scratch_shapes=[pltpu.VMEM(like.shape, F32) for like in likes[:4]]
        + [
            pltpu.VMEM((HALF, HALF), F32),
            pltpu.VMEM((4, ROWS, 2 * HALF), F32),
            pltpu.VMEM((16, 2 * HALF), F32),
            pltpu.VMEM((16, HALF), F32),
            pltpu.VMEM((16, 8 * HALF), F32),
            pltpu.SemaphoreType.DMA((15,)),
        ],
        compiler_params=pltpu.CompilerParams(vmem_limit_bytes=24 << 20),
        name="gradients",
    )(*sums, embed, conv, mix, out_weight, picks_t, swap)


def on_device(
    tokens, dilations, embed, conv_weight, mix_weight, gate_bias, out_weight, cot_fwd, cot_rev
):
    count = lax.axis_size("seq")
    picks, picks_t, swap = [jnp.asarray(value, BF16) for value in selectors()]
    weights = (embed, conv_weight, mix_weight, gate_bias, out_weight)
    sums = main(
        tokens.reshape(tokens.shape[0] // 128, 128), dilations, *weights, cot_fwd, cot_rev, picks, swap, count
    )
    return tuple(gradients(sums, *weights, picks_t, swap))


def solution(mesh):
    in_specs = (
        P(("dp", "seq")),
        P(),
        P(),
        P(),
        P(),
        P(),
        P(),
        P(("dp", "seq"), None),
        P(("dp", "seq"), None),
    )
    out_specs = (
        P(("dp", "seq"), None),
        P(("dp", "seq"), None),
        P("dp", None),
        P("dp", None, None, None),
        P("dp", None, None),
        P("dp", None),
        P("dp", None, None),
    )
    return jax.shard_map(
        on_device, mesh=mesh, in_specs=in_specs, out_specs=out_specs, check_vma=False
    )
```

```python
import functools

import jax
import jax.numpy as jnp
import numpy as np
from jax import lax
from jax.experimental import pallas as pl
from jax.experimental.pallas import tpu as pltpu
from jax.sharding import PartitionSpec as P

MESH = pl.DeviceIdType.MESH
ROWS = 128
INNER = 64
EDGE = 16
KEPT = INNER + 2 * EDGE
HALF = 256
GATE_PIECE = 56
EDGE_PIECE = 32
OUT_PIECE = 32
SENT = GATE_PIECE + EDGE_PIECE
OUTSIDE = 4
NONE = 255
F32 = jnp.float32
BF16 = jnp.bfloat16
VMEM = pl.BlockSpec(memory_space=pltpu.VMEM)
HBM = pl.BlockSpec(memory_space=pltpu.HBM)


def selectors():
    row = np.arange(ROWS)
    live = row < KEPT
    inner, before = row < INNER, row < INNER + EDGE
    low = row % 4
    own = (row // 4) % 4
    left = np.where(inner, row // 16, np.where(before, OUTSIDE, low))
    right = np.where(inner | before, low, OUTSIDE)
    picks = np.zeros((ROWS, 16), np.float32)
    for base in range(4):
        picks[:, base] = live & (left == base)
        picks[:, 4 + base] = live & (own == base)
        picks[:, 8 + base] = live & (right == base)
        picks[:, 12 + base] = live & (own == 3 - base)
    flipped = np.array([3, 2, 1, 0, OUTSIDE])
    other = code_of(flipped[right], flipped[own], flipped[left], np.where)
    swap = (np.where(live, other, row)[:, None] == row).astype(np.float32)
    return picks, picks.T.copy(), swap


def code_of(left, own, right, where):
    inner = left * 16 + own * 4 + right
    return where(
        left == OUTSIDE, INNER + own * 4 + right, where(right == OUTSIDE, INNER + EDGE + own * 4 + left, inner)
    )


def split(value):
    high = value.astype(BF16)
    return high, (value - high.astype(F32)).astype(BF16)


def dot(a, b, dims=((1,), (0,))):
    return lax.dot_general(a, b, (dims, ((), ())), preferred_element_type=F32)


def dot2(exact, parts, dims=((1,), (0,))):
    return dot(exact, parts[0], dims) + dot(exact, parts[1], dims)


def dot3(a, b, dims=((1,), (0,))):
    return dot(a[0], b[0], dims) + (dot(a[0], b[1], dims) + dot(a[1], b[0], dims))


NT = ((1,), (1,))
TN = ((0,), (0,))


def sigmoid(value):
    return 0.5 * jnp.tanh(0.5 * value) + 0.5


def exclusive(value, bits):
    total = 0
    for bit in (1, 2, 4):
        digit = lax.rem(lax.div(value, bit), 2)
        total = total + bit * (1 - digit if bits & bit else digit)
    return total


def tables(embed_ref, conv_ref, mix_ref, bias_ref, out_ref, picks, swap, wide, high, low):
    wide[...] = jnp.zeros_like(wide)
    wide[16:20, :HALF] = embed_ref[...]
    embed = split(wide[16:24, :HALF])
    for at in range(4):
        weight = conv_ref[0, at] if at < 3 else mix_ref[0]
        wide[4 * at : 4 * at + 4, :] = dot3(embed, split(weight))[:4]
    mixed = dot2(picks, split(wide[:16, :])) + bias_ref[0:1, :]
    tanh = jnp.tanh(mixed[:, :HALF])
    sig = sigmoid(mixed[:, HALF:])
    wide[...] = jnp.zeros_like(wide)
    wide[4:8, :HALF] = embed_ref[...]
    table = dot2(picks, split(wide[:16, :HALF])) + dot3(split(tanh * sig), split(out_ref[0]))
    parts = split(table)
    swapped = [dot(swap, part).astype(BF16) for part in parts]
    weights = [split(conv_ref[1, at]) for at in range(3)]
    for at in range(3):
        product = dot3(parts, weights[at])
        if at == 1:
            product = product + dot3(swapped, split(mix_ref[1])) + bias_ref[1:2, :]
        high[ROWS * at : ROWS * at + ROWS, :], low[ROWS * at : ROWS * at + ROWS, :] = split(product)
    return table, tanh, sig


def beside(window):
    return jnp.concatenate([window[7:15, :], window[8:16, :], window[9:17, :]], axis=1).astype(BF16)


def chosen(length, other, sources):
    row = lax.broadcasted_iota(jnp.int32, (length, 128), 0)
    column = lax.broadcasted_iota(jnp.int32, (length, 128), 1)
    return jnp.concatenate(
        [jnp.where(row == source(column), 1.0, 0.0).astype(BF16) for source in sources], axis=1
    )


def chosen_t(length, sources):
    row = lax.broadcasted_iota(jnp.int32, (128, length), 0)
    column = lax.broadcasted_iota(jnp.int32, (128, length), 1)
    return jnp.concatenate(
        [jnp.where(column == source(row), 1.0, 0.0).astype(BF16) for source in sources], axis=0
    )


def far_sources(far, strand):
    if strand == 0:
        return [lambda at: 128 + at - far, lambda at: 128 + at, lambda at: 128 + at + far]
    return [lambda at: 255 - at + far, lambda at: 255 - at, lambda at: 255 - at - far]


def turned(base):
    return jnp.where(base == OUTSIDE, float(OUTSIDE), 3.0 - base)


def main_kernel(
    tokens_hbm,
    dilations_hbm,
    embed_hbm,
    conv_hbm,
    mix_hbm,
    bias_hbm,
    out_weight_hbm,
    cot_fwd_hbm,
    cot_rev_hbm,
    picks_hbm,
    swap_hbm,
    gate_ref,
    out_ref,
    result_ref,
    table_t_ref,
    hidden_t_ref,
    tanh_ref,
    sig_ref,
    dilations,
    embed_ref,
    conv_ref,
    mix_ref,
    bias_ref,
    out_weight_ref,
    cot_ref,
    picks_ref,
    swap_ref,
    landed,
    window,
    wide,
    high,
    low,
    hot,
    hot_t,
    hidden_parts,
    cot_parts,
    grad_parts,
    back_ref,
    part_gate,
    part_out,
    part_edge,
    paired_gate,
    paired_out,
    summed_gate,
    summed_out,
    arrived_gate,
    arrived_out,
    load_sems,
    token_sems,
    sent_sems,
    pair_sems,
    chip_sems,
    spread_sems,
    twin_sems,
    edge_sems,
):
    me = lax.axis_index("seq")
    count = landed.shape[0] - 2
    length = cot_fwd_hbm.shape[0]
    barrier = pltpu.get_barrier_semaphore()
    peers = [lax.rem(me + step, count) for step in range(1, count)]
    for peer in peers:
        pl.semaphore_signal(barrier, inc=1, device_id={"seq": peer}, device_id_type=MESH)

    moves = [
        (embed_hbm, embed_ref),
        (conv_hbm, conv_ref),
        (mix_hbm, mix_ref),
        (bias_hbm, bias_ref),
        (out_weight_hbm, out_weight_ref),
        (picks_hbm, picks_ref),
        (swap_hbm, swap_ref),
        (cot_fwd_hbm, cot_ref.at[pl.ds(0, length)]),
        (cot_rev_hbm, cot_ref.at[pl.ds(length, length)]),
        (dilations_hbm, dilations),
        (tokens_hbm, landed.at[me + 1]),
    ]
    loads = []
    for at, (source, landing) in enumerate(moves):
        loads.append(pltpu.make_async_copy(source, landing, load_sems.at[at]))
        loads[-1].start()
    edge = jnp.full(landed.shape[1:], OUTSIDE, jnp.int32)
    landed[0] = edge
    landed[count + 1] = edge
    window[...] = jnp.zeros_like(window)
    part_edge[...] = jnp.zeros_like(part_edge)

    def remote(source, landing, send_sem, recv_sem, target):
        return pltpu.make_async_remote_copy(
            src_ref=source,
            dst_ref=landing,
            send_sem=send_sem,
            recv_sem=recv_sem,
            device_id={"seq": target},
            device_id_type=MESH,
        )

    pl.semaphore_wait(barrier, count - 1)
    flip = count - 1 - me
    apart = flip - me
    routes = (
        (me + 1, me < count - 1, me - 1, me > 0),
        (me - 1, me > 0, me + 1, me < count - 1),
        (flip, apart * apart != 1, flip, apart * apart != 1),
        (flip - 1, jnp.logical_and(flip > 0, apart != 1), flip - 1, jnp.logical_and(flip > 0, apart != 1)),
        (
            flip + 1,
            jnp.logical_and(flip < count - 1, apart != -1),
            flip + 1,
            jnp.logical_and(flip < count - 1, apart != -1),
        ),
    )

    def token_copy(at, source, landing):
        target = lax.rem(routes[at][0] + count, count)
        return remote(source, landing, token_sems.at[0, at], token_sems.at[1, at], target)

    for at in range(5):

        @pl.when(routes[at][1])
        def _():
            token_copy(at, tokens_hbm, landed.at[me + 1]).start()


    for load in loads:
        load.wait()
    near, far = dilations[0], dilations[1]
    table, tanh, sig = tables(
        embed_ref, conv_ref, mix_ref, bias_ref, out_weight_ref, picks_ref[...], swap_ref[...], wide, high, low
    )
    tanh_ref[...], sig_ref[...] = tanh, sig
    table_parts = split(table)
    for ref, value in ((table_t_ref, table), (hidden_t_ref, tanh * sig)):
        upper, lower = split(jnp.transpose(value))
        ref[:, :ROWS], ref[:, ROWS : 2 * ROWS], ref[:, 2 * ROWS :] = upper, upper, lower
    out_parts = split(out_weight_ref[1])
    for block in range(4):
        rows = pl.ds(256 * block, 256)
        cots = split(cot_ref[rows, :])
        cot_parts[0, rows, :], cot_parts[1, rows, :] = cots
        back_ref[rows, :] = dot3(cots, out_parts, NT)

    for at in range(5):

        @pl.when(routes[at][3])
        def _():
            landing = landed.at[routes[at][2] + 1]
            token_copy(at, landing, landing).wait_recv()

    near_move = chosen(384, 256, [lambda at: 128 + at - near, lambda at: 128 + at + near])
    lane = lax.broadcasted_iota(jnp.int32, (128, 128), 1).astype(F32)
    sub = lax.broadcasted_iota(jnp.int32, (128, 128), 0).astype(F32)
    for strand in range(2):
        block = me if strand == 0 else count - 1 - me
        window[0, 8:10, :] = landed[block][2:4].astype(F32)
        window[0, 10:14, :] = landed[block + 1].astype(F32)
        window[0, 14:16, :] = landed[block + 2][0:2].astype(F32)
        own = window[0, 8:16, :]
        moved = dot(beside(window.at[0]), near_move)
        lower, upper = moved[:, :128], moved[:, 128:]
        if strand == 0:
            code = code_of(lower, own, upper, jnp.where)
        else:
            code = code_of(turned(upper), 3.0 - own, turned(lower), jnp.where)
        window[1, 8:16, :] = jnp.where(own == OUTSIDE, float(NONE), code)
        codes = beside(window.at[1])
        sources = far_sources(far, strand)
        across = dot(codes, chosen(384, 384, sources))
        down = dot(chosen_t(384, sources), codes, NT)
        for tap in range(3):
            taps = slice(128 * tap, 128 * tap + 128)
            for row in range(4):
                at = row + 2 if strand == 0 else 5 - row
                places = slice(512 * strand + 128 * row, 512 * strand + 128 * row + 128)
                hot[places, taps] = jnp.where(down[taps, at : at + 1] == lane, 1.0, 0.0).astype(BF16)
                hot_t[KEPT * tap : KEPT * tap + KEPT, places] = jnp.where(
                    across[at : at + 1, taps] == sub[:KEPT], 1.0, 0.0
                ).astype(BF16)

    for block in range(4):
        rows = pl.ds(256 * block, 256)
        mixed = dot2(hot[rows, :], (high[...], low[...]))
        act, gate = jnp.tanh(mixed[:, :HALF]), sigmoid(mixed[:, HALF:])
        hidden = split(act * gate)
        scaled = back_ref[rows, :] * gate
        grad_act = split(scaled * (1.0 - act * act))
        grad_gate = split(scaled * act * (1.0 - gate))
        for part in range(2):
            hidden_parts[part, rows, :] = hidden[part]
            grad_parts[part, rows, :HALF] = grad_act[part]
            grad_parts[part, rows, HALF:] = grad_gate[part]

    core = lax.rem(me, 2)
    chip = lax.div(me, 2)
    twin = me + 1 - 2 * core
    chips = [exclusive(chip, bits) for bits in range(8)]
    partners = [2 * other + core for other in chips]
    order = (7, 5, 6, 4, 2, 3, 1, 0)
    stages = (
        (GATE_PIECE, SENT, part_gate, paired_gate, summed_gate, arrived_gate, gate_ref),
        (OUT_PIECE, OUT_PIECE, part_out, paired_out, summed_out, arrived_out, out_ref),
    )
    first = {}
    source_chip = 7 * core
    is_source = chip == source_chip

    def rows_of(size, device):
        return pl.ds(pl.multiple_of(device * size, 8), size)

    def landing_of(stage, device):
        return stages[stage][6].at[rows_of(stages[stage][1], device)]

    def edge_landing(device):
        return gate_ref.at[pl.ds(pl.multiple_of(device * SENT + GATE_PIECE, 8), EDGE_PIECE)]

    def edge_copy(at):
        return pltpu.make_async_remote_copy(
            src_ref=part_edge.at[rows_of(EDGE_PIECE, chips[at])],
            dst_ref=edge_landing(partners[at]),
            send_sem=edge_sems.at[0],
            recv_sem=edge_sems.at[1],
            device_id={"seq": partners[at]},
            device_id_type=MESH,
        )

    def pair(stage):
        size, _, part, paired, _, _, _ = stages[stage]
        for at in order:
            source = part.at[rows_of(size, 2 * chips[at] + 1 - core)]
            first[stage, at] = remote(
                source, paired.at[at], sent_sems.at[stage], pair_sems.at[8 * stage + at], twin
            )
            first[stage, at].start()

    def scatter(stage):
        size, _, part, paired, summed, arrived, _ = stages[stage]
        for at in order:
            first[stage, at].wait_recv()
            summed[at] = paired[at] + part[rows_of(size, partners[at]), :]
            if at:
                remote(
                    summed.at[at], arrived.at[at], sent_sems.at[2 + stage], chip_sems.at[stage], partners[at]
                ).start()

    def spread(stage):
        size, sent, _, _, summed, arrived, out = stages[stage]
        whole = arrived.at[pl.ds(1, 7)]
        remote(whole, whole, sent_sems.at[2 + stage], chip_sems.at[stage], twin).wait_recv()
        total = summed[0]
        for at in order[:-1]:
            total = total + arrived[at]
        out[pl.ds(pl.multiple_of(me * sent, 8), size), :] = total
        mine = landing_of(stage, me)
        for at in order[:-1]:
            remote(
                mine, mine, sent_sems.at[4 + stage], spread_sems.at[8 * stage + at], partners[at]
            ).start()
        remote(mine, mine, sent_sems.at[6 + stage], twin_sems.at[stage], twin).start()

    def forward(stage):
        for at in order[:-1]:
            landing = landing_of(stage, partners[at])
            remote(
                landing, landing, sent_sems.at[4 + stage], spread_sems.at[8 * stage + at], partners[at]
            ).wait_recv()
            remote(landing, landing, sent_sems.at[6 + stage], twin_sems.at[stage], twin).start()

    def finish(stage):
        size, sent, part, _, _, _, out = stages[stage]
        whole = out.at[pl.ds(0, 8 * sent)]
        remote(whole, whole, sent_sems.at[6 + stage], twin_sems.at[stage], twin).wait_recv()
        for step, (ref, rows) in enumerate(((part, 8 * size), (part, 7 * size), (out, 7 * sent), (out, 8 * sent))):
            view = ref.at[pl.ds(0, rows)]
            remote(view, view, sent_sems.at[2 * step + stage], twin_sems.at[stage], twin).wait_send()

    cot_pair = (cot_parts[0], cot_parts[1])
    sums = dot2(hot_t[...], (grad_parts[0], grad_parts[1]))
    cot_sums = dot2(hot_t[KEPT : 2 * KEPT, :], cot_pair)
    columns = [
        sums[KEPT * tap : KEPT * tap + KEPT, 128 * at : 128 * at + 128] for tap in range(3) for at in range(4)
    ] + [cot_sums[:, :128], cot_sums[:, 128:]]
    for at, column in enumerate(columns):
        part_gate[INNER * at : INNER * at + INNER, :] = column[:INNER]
    pair(0)
    for at, column in enumerate(columns):
        part_edge[EDGE * at : EDGE * at + EDGE, :] = jnp.where(
            me == 0, column[INNER : INNER + EDGE], column[INNER + EDGE :]
        )

    @pl.when(is_source)
    def _():
        for at in order[:-1]:
            edge_copy(at).start()
        own_rows = pl.ds(pl.multiple_of(me * SENT + GATE_PIECE, 8), EDGE_PIECE)
        gate_ref[own_rows, :] = part_edge[rows_of(EDGE_PIECE, chip), :]

    product = dot3((hidden_parts[0], hidden_parts[1]), cot_pair, TN)
    part_out[:HALF, :], part_out[HALF:, :] = product[:, :128], product[:, 128:]
    scatter(0)
    pair(1)
    scatter(1)
    for block in range(4):
        rows = pl.ds(256 * block, 256)
        result_ref[rows, :] = dot2(hot[rows, ROWS : 2 * ROWS], table_parts) + dot3(
            (hidden_parts[0, rows, :], hidden_parts[1, rows, :]), out_parts
        )

    @pl.when(jnp.logical_not(is_source))
    def _():
        edge_copy(0).wait_recv()

    spread(0)
    spread(1)
    forward(0)
    forward(1)
    finish(0)
    finish(1)
    for at in range(5):

        @pl.when(routes[at][1])
        def _():
            token_copy(at, tokens_hbm, landed.at[me + 1]).wait_send()

    @pl.when(is_source)
    def _():
        view = part_edge.at[pl.ds(0, 7 * EDGE_PIECE)]
        remote(view, view, edge_sems.at[0], edge_sems.at[1], twin).wait_send()


def main(tokens, dilations, embed, conv, mix, bias, out_weight, cot_fwd, cot_rev, picks, swap, count):
    length = cot_fwd.shape[0]
    shape = lambda *dims: jax.ShapeDtypeStruct(dims, F32)
    like = lambda array: pltpu.VMEM(array.shape, array.dtype)
    sems = pltpu.SemaphoreType.DMA
    return pl.pallas_call(
        main_kernel,
        out_shape=[
            shape(count * SENT, 128),
            shape(count * OUT_PIECE, 128),
            shape(2 * length, HALF),
            jax.ShapeDtypeStruct((HALF, 3 * ROWS), BF16),
            jax.ShapeDtypeStruct((HALF, 3 * ROWS), BF16),
            shape(ROWS, HALF),
            shape(ROWS, HALF),
        ],
        in_specs=[HBM] * 11,
        out_specs=[VMEM] * 7,
        scratch_shapes=[
            pltpu.SMEM(dilations.shape, jnp.int32),
            like(embed),
            like(conv),
            like(mix),
            like(bias),
            like(out_weight),
            pltpu.VMEM((2 * length, HALF), F32),
            like(picks),
            like(swap),
            pltpu.VMEM((count + 2,) + tokens.shape, jnp.int32),
            pltpu.VMEM((2, 24, 128), F32),
            pltpu.VMEM((24, 2 * HALF), F32),
            pltpu.VMEM((3 * ROWS, 2 * HALF), BF16),
            pltpu.VMEM((3 * ROWS, 2 * HALF), BF16),
            pltpu.VMEM((2 * length, 3 * ROWS), BF16),
            pltpu.VMEM((3 * KEPT, 2 * length), BF16),
            pltpu.VMEM((2, 2 * length, HALF), BF16),
            pltpu.VMEM((2, 2 * length, HALF), BF16),
            pltpu.VMEM((2, 2 * length, 2 * HALF), BF16),
            pltpu.VMEM((2 * length, HALF), F32),
            pltpu.VMEM((count * GATE_PIECE, 128), F32),
            pltpu.VMEM((count * OUT_PIECE, 128), F32),
            pltpu.VMEM((8 * EDGE_PIECE, 128), F32),
        ]
        + [pltpu.VMEM((8, size, 128), F32) for _ in range(3) for size in (GATE_PIECE, OUT_PIECE)]
        + [
            sems((11,)),
            sems((2, 5)),
            sems((8,)),
            sems((16,)),
            sems((2,)),
            sems((16,)),
            sems((2,)),
            sems((2,)),
        ],
        compiler_params=pltpu.CompilerParams(
            collective_id=0, has_side_effects=True, vmem_limit_bytes=40 << 20
        ),
        name="local_work_and_sums",
    )(
        *[
            pltpu.with_memory_space_constraint(array, pltpu.HBM)
            for array in (
                tokens, dilations, embed, conv, mix, bias, out_weight, cot_fwd, cot_rev, picks, swap
            )
        ]
    )


def pieces_of(begin, rows, piece, place):
    at = begin
    while at < begin + rows:
        device, inside = at // piece, at % piece
        length = min(piece - inside, begin + rows - at)
        yield at - begin, place(device) + inside, length
        at += length


def gradient_kernel(
    gate_ref,
    out_ref,
    result_ref,
    table_t_ref,
    hidden_t_ref,
    tanh_ref,
    sig_ref,
    embed_ref,
    conv_ref,
    mix_ref,
    out_weight_ref,
    picks_t_ref,
    swap_ref,
    out_fwd_hbm,
    out_rev_hbm,
    grad_embed_hbm,
    grad_conv_hbm,
    grad_mix_hbm,
    grad_bias_hbm,
    grad_out_hbm,
    grad_embed_ref,
    grad_conv_ref,
    grad_mix_ref,
    grad_bias_ref,
    grad_out_ref,
    sums,
    wide,
    rows_left,
    rows_right,
    sems,
):
    length = out_fwd_hbm.shape[0]
    stores = []

    def store(source, landing):
        stores.append(pltpu.make_async_copy(source, landing, sems.at[len(stores)]))
        stores[-1].start()

    store(result_ref.at[pl.ds(0, length)], out_fwd_hbm)
    store(result_ref.at[pl.ds(length, length)], out_rev_hbm)
    for at in range(2):
        store(out_ref.at[pl.ds(HALF * at, HALF)], grad_out_hbm.at[1, :, pl.ds(128 * at, 128)])
    sums[:, KEPT:, :] = jnp.zeros((4, ROWS - KEPT, 2 * HALF), F32)
    for at in range(14):
        tap, columns = at // 4, pl.ds(128 * (at % 4), 128)
        runs = list(pieces_of(INNER * at, INNER, GATE_PIECE, lambda device: SENT * device))
        for side in range(2):
            for offset, address, size in pieces_of(
                EDGE * at, EDGE, EDGE_PIECE, lambda chip: SENT * (2 * chip + side) + GATE_PIECE
            ):
                runs.append((INNER + EDGE * side + offset, address, size))
        for offset, address, size in runs:
            sums[tap, pl.ds(offset, size), columns] = gate_ref[pl.ds(address, size), :]
    grad_bias_ref[1:2, :] = jnp.sum(sums[1], axis=0, keepdims=True)

    swap = swap_ref[...]
    grad = sums[3, :, :HALF]
    parts = [split(sums[tap]) for tap in range(3)]
    parts.append([dot(swap, part).astype(BF16) for part in parts[1]])
    table_t = table_t_ref[...]
    for at in range(4):
        upper, lower = parts[at]
        product = dot(table_t, jnp.concatenate([upper, lower, upper], axis=0))
        if at < 3:
            grad_conv_ref[1, at] = product
            store(grad_conv_ref.at[1, at], grad_conv_hbm.at[1, at])
        else:
            grad_mix_ref[1] = product
            store(grad_mix_ref.at[1], grad_mix_hbm.at[1])
        grad = grad + dot3(parts[at], split(conv_ref[1, at] if at < 3 else mix_ref[1]), NT)

    grads = split(grad)
    tanh, sig = tanh_ref[...], sig_ref[...]
    back = dot3(grads, split(out_weight_ref[0]), NT) * sig
    act, gate = back * (1.0 - tanh * tanh), back * tanh * (1.0 - sig)
    picks_t = picks_t_ref[...]
    wide[:, :HALF] = dot2(picks_t, split(act))
    wide[:, HALF:] = dot2(picks_t, split(gate))
    bases = split(embed_ref[...])
    rows_left[...] = jnp.zeros_like(rows_left)
    rows_right[...] = jnp.zeros_like(rows_right)
    pieces = [split(wide[4 * at : 4 * at + 4, :]) for at in range(4)]
    for at, part in enumerate((0, 0, 1)):
        rows_left[4 * at : 4 * at + 4, :] = bases[part].astype(F32)
    for at, part in enumerate((0, 1, 0)):
        for tap in range(4):
            rows_right[4 * at : 4 * at + 4, 512 * tap : 512 * tap + 512] = pieces[tap][part].astype(F32)
    left = rows_left[...].astype(BF16)
    for at in range(4):
        product = dot(left, rows_right[:, 512 * at : 512 * at + 512].astype(BF16), TN)
        if at < 3:
            grad_conv_ref[0, at] = product
            store(grad_conv_ref.at[0, at], grad_conv_hbm.at[0, at])
        else:
            grad_mix_ref[0] = product
            store(grad_mix_ref.at[0], grad_mix_hbm.at[0])
    grad_out_ref[...] = dot(hidden_t_ref[...], jnp.concatenate([grads[0], grads[1], grads[0]], axis=0))
    store(grad_out_ref, grad_out_hbm.at[0])
    grad_bias_ref[0:1, :HALF] = jnp.sum(act, axis=0, keepdims=True)
    grad_bias_ref[0:1, HALF:] = jnp.sum(gate, axis=0, keepdims=True)
    store(grad_bias_ref, grad_bias_hbm)
    embed_grad = dot2(picks_t, grads)[4:8]
    for at in range(4):
        embed_grad = embed_grad + dot3(pieces[at], split(conv_ref[0, at] if at < 3 else mix_ref[0]), NT)
    grad_embed_ref[...] = embed_grad
    store(grad_embed_ref, grad_embed_hbm)
    for copy in stores:
        copy.wait()


def gradients(sums, embed, conv, mix, bias, out_weight, picks_t, swap):
    half_result = jax.ShapeDtypeStruct((sums[2].shape[0] // 2, HALF), F32)
    likes = (embed, conv, mix, bias, out_weight)
    return pl.pallas_call(
        gradient_kernel,
        out_shape=[half_result] * 2 + [jax.ShapeDtypeStruct(like.shape, F32) for like in likes],
        in_specs=[VMEM] * 13,
        out_specs=[HBM] * 7,
        scratch_shapes=[pltpu.VMEM(like.shape, F32) for like in likes[:4]]
        + [
            pltpu.VMEM((HALF, HALF), F32),
            pltpu.VMEM((4, ROWS, 2 * HALF), F32),
            pltpu.VMEM((16, 2 * HALF), F32),
            pltpu.VMEM((16, HALF), F32),
            pltpu.VMEM((16, 8 * HALF), F32),
            pltpu.SemaphoreType.DMA((15,)),
        ],
        compiler_params=pltpu.CompilerParams(vmem_limit_bytes=24 << 20),
        name="gradients",
    )(*sums, embed, conv, mix, out_weight, picks_t, swap)


def on_device(
    tokens, dilations, embed, conv_weight, mix_weight, gate_bias, out_weight, cot_fwd, cot_rev
):
    count = lax.axis_size("seq")
    picks, picks_t, swap = [jnp.asarray(value, BF16) for value in selectors()]
    weights = (embed, conv_weight, mix_weight, gate_bias, out_weight)
    sums = main(
        tokens.reshape(tokens.shape[0] // 128, 128), dilations, *weights, cot_fwd, cot_rev, picks, swap, count
    )
    return tuple(gradients(sums, *weights, picks_t, swap))


def solution(mesh):
    in_specs = (
        P(("dp", "seq")),
        P(),
        P(),
        P(),
        P(),
        P(),
        P(),
        P(("dp", "seq"), None),
        P(("dp", "seq"), None),
    )
    out_specs = (
        P(("dp", "seq"), None),
        P(("dp", "seq"), None),
        P("dp", None),
        P("dp", None, None, None),
        P("dp", None, None),
        P("dp", None),
        P("dp", None, None),
    )
    return jax.shard_map(
        on_device, mesh=mesh, in_specs=in_specs, out_specs=out_specs, check_vma=False
    )
```

```python
import functools

import jax
import jax.numpy as jnp
import numpy as np
from jax import lax
from jax.experimental import pallas as pl
from jax.experimental.pallas import tpu as pltpu
from jax.sharding import PartitionSpec as P

MESH = pl.DeviceIdType.MESH
ROWS = 128
INNER = 64
EDGE = 16
KEPT = INNER + 2 * EDGE
HALF = 256
GATE_PIECE = 56
EDGE_PIECE = 32
OUT_PIECE = 32
SENT = GATE_PIECE + EDGE_PIECE
OUTSIDE = 4
NONE = 255
F32 = jnp.float32
BF16 = jnp.bfloat16
VMEM = pl.BlockSpec(memory_space=pltpu.VMEM)
HBM = pl.BlockSpec(memory_space=pltpu.HBM)


def selectors():
    row = np.arange(ROWS)
    live = row < KEPT
    inner, before = row < INNER, row < INNER + EDGE
    low = row % 4
    own = (row // 4) % 4
    left = np.where(inner, row // 16, np.where(before, OUTSIDE, low))
    right = np.where(inner | before, low, OUTSIDE)
    picks = np.zeros((ROWS, 16), np.float32)
    for base in range(4):
        picks[:, base] = live & (left == base)
        picks[:, 4 + base] = live & (own == base)
        picks[:, 8 + base] = live & (right == base)
        picks[:, 12 + base] = live & (own == 3 - base)
    flipped = np.array([3, 2, 1, 0, OUTSIDE])
    other = code_of(flipped[right], flipped[own], flipped[left], np.where)
    swap = (np.where(live, other, row)[:, None] == row).astype(np.float32)
    return picks, picks.T.copy(), swap


def code_of(left, own, right, where):
    inner = left * 16 + own * 4 + right
    return where(
        left == OUTSIDE, INNER + own * 4 + right, where(right == OUTSIDE, INNER + EDGE + own * 4 + left, inner)
    )


def split(value):
    high = value.astype(BF16)
    return high, (value - high.astype(F32)).astype(BF16)


def dot(a, b, dims=((1,), (0,))):
    return lax.dot_general(a, b, (dims, ((), ())), preferred_element_type=F32)


def dot2(exact, parts, dims=((1,), (0,))):
    return dot(exact, parts[0], dims) + dot(exact, parts[1], dims)


def dot3(a, b, dims=((1,), (0,))):
    return dot(a[0], b[0], dims) + (dot(a[0], b[1], dims) + dot(a[1], b[0], dims))


NT = ((1,), (1,))
TN = ((0,), (0,))


def sigmoid(value):
    return 0.5 * jnp.tanh(0.5 * value) + 0.5


def exclusive(value, bits):
    total = 0
    for bit in (1, 2, 4):
        digit = lax.rem(lax.div(value, bit), 2)
        total = total + bit * (1 - digit if bits & bit else digit)
    return total


def tables(embed_ref, conv_ref, mix_ref, bias_ref, out_ref, picks, swap, wide, high, low):
    wide[...] = jnp.zeros_like(wide)
    wide[16:20, :HALF] = embed_ref[...]
    embed = split(wide[16:24, :HALF])
    for at in range(4):
        weight = conv_ref[0, at] if at < 3 else mix_ref[0]
        wide[4 * at : 4 * at + 4, :] = dot3(embed, split(weight))[:4]
    mixed = dot2(picks, split(wide[:16, :])) + bias_ref[0:1, :]
    tanh = jnp.tanh(mixed[:, :HALF])
    sig = sigmoid(mixed[:, HALF:])
    wide[...] = jnp.zeros_like(wide)
    wide[4:8, :HALF] = embed_ref[...]
    table = dot2(picks, split(wide[:16, :HALF])) + dot3(split(tanh * sig), split(out_ref[0]))
    parts = split(table)
    swapped = [dot(swap, part).astype(BF16) for part in parts]
    weights = [split(conv_ref[1, at]) for at in range(3)]
    for at in range(3):
        product = dot3(parts, weights[at])
        if at == 1:
            product = product + dot3(swapped, split(mix_ref[1])) + bias_ref[1:2, :]
        high[ROWS * at : ROWS * at + ROWS, :], low[ROWS * at : ROWS * at + ROWS, :] = split(product)
    return table, tanh, sig


def beside(window):
    return jnp.concatenate([window[7:15, :], window[8:16, :], window[9:17, :]], axis=1).astype(BF16)


def chosen(length, other, sources):
    row = lax.broadcasted_iota(jnp.int32, (length, 128), 0)
    column = lax.broadcasted_iota(jnp.int32, (length, 128), 1)
    return jnp.concatenate(
        [jnp.where(row == source(column), 1.0, 0.0).astype(BF16) for source in sources], axis=1
    )


def chosen_t(length, sources):
    row = lax.broadcasted_iota(jnp.int32, (128, length), 0)
    column = lax.broadcasted_iota(jnp.int32, (128, length), 1)
    return jnp.concatenate(
        [jnp.where(column == source(row), 1.0, 0.0).astype(BF16) for source in sources], axis=0
    )


def far_sources(far, strand):
    if strand == 0:
        return [lambda at: 128 + at - far, lambda at: 128 + at, lambda at: 128 + at + far]
    return [lambda at: 255 - at + far, lambda at: 255 - at, lambda at: 255 - at - far]


def turned(base):
    return jnp.where(base == OUTSIDE, float(OUTSIDE), 3.0 - base)


def main_kernel(
    tokens_hbm,
    dilations_hbm,
    embed_hbm,
    conv_hbm,
    mix_hbm,
    bias_hbm,
    out_weight_hbm,
    cot_fwd_hbm,
    cot_rev_hbm,
    picks_hbm,
    swap_hbm,
    gate_ref,
    out_ref,
    result_ref,
    table_t_ref,
    hidden_t_ref,
    tanh_ref,
    sig_ref,
    weight_parts_ref,
    out_parts_ref,
    dilations,
    embed_ref,
    conv_ref,
    mix_ref,
    bias_ref,
    out_weight_ref,
    cot_ref,
    picks_ref,
    swap_ref,
    landed,
    window,
    wide,
    high,
    low,
    hot,
    hot_t,
    hidden_parts,
    cot_parts,
    grad_parts,
    back_ref,
    part_gate,
    part_out,
    part_edge,
    paired_gate,
    paired_out,
    summed_gate,
    summed_out,
    arrived_gate,
    arrived_out,
    load_sems,
    token_sems,
    sent_sems,
    pair_sems,
    chip_sems,
    spread_sems,
    twin_sems,
    edge_sems,
):
    me = lax.axis_index("seq")
    count = landed.shape[0] - 2
    length = cot_fwd_hbm.shape[0]
    barrier = pltpu.get_barrier_semaphore()
    peers = [lax.rem(me + step, count) for step in range(1, count)]
    for peer in peers:
        pl.semaphore_signal(barrier, inc=1, device_id={"seq": peer}, device_id_type=MESH)

    moves = [
        (embed_hbm, embed_ref),
        (conv_hbm, conv_ref),
        (mix_hbm, mix_ref),
        (bias_hbm, bias_ref),
        (out_weight_hbm, out_weight_ref),
        (picks_hbm, picks_ref),
        (swap_hbm, swap_ref),
        (cot_fwd_hbm, cot_ref.at[pl.ds(0, length)]),
        (cot_rev_hbm, cot_ref.at[pl.ds(length, length)]),
        (dilations_hbm, dilations),
        (tokens_hbm, landed.at[me + 1]),
    ]
    loads = []
    for at, (source, landing) in enumerate(moves):
        loads.append(pltpu.make_async_copy(source, landing, load_sems.at[at]))
        loads[-1].start()
    edge = jnp.full(landed.shape[1:], OUTSIDE, jnp.int32)
    landed[0] = edge
    landed[count + 1] = edge
    window[...] = jnp.zeros_like(window)
    part_edge[...] = jnp.zeros_like(part_edge)

    def remote(source, landing, send_sem, recv_sem, target):
        return pltpu.make_async_remote_copy(
            src_ref=source,
            dst_ref=landing,
            send_sem=send_sem,
            recv_sem=recv_sem,
            device_id={"seq": target},
            device_id_type=MESH,
        )

    pl.semaphore_wait(barrier, count - 1)
    flip = count - 1 - me
    apart = flip - me
    routes = (
        (me + 1, me < count - 1, me - 1, me > 0),
        (me - 1, me > 0, me + 1, me < count - 1),
        (flip, apart * apart != 1, flip, apart * apart != 1),
        (flip - 1, jnp.logical_and(flip > 0, apart != 1), flip - 1, jnp.logical_and(flip > 0, apart != 1)),
        (
            flip + 1,
            jnp.logical_and(flip < count - 1, apart != -1),
            flip + 1,
            jnp.logical_and(flip < count - 1, apart != -1),
        ),
    )

    def token_copy(at, source, landing):
        target = lax.rem(routes[at][0] + count, count)
        return remote(source, landing, token_sems.at[0, at], token_sems.at[1, at], target)

    for at in range(5):

        @pl.when(routes[at][1])
        def _():
            token_copy(at, tokens_hbm, landed.at[me + 1]).start()


    for load in loads:
        load.wait()
    near, far = dilations[0], dilations[1]
    table, tanh, sig = tables(
        embed_ref, conv_ref, mix_ref, bias_ref, out_weight_ref, picks_ref[...], swap_ref[...], wide, high, low
    )
    tanh_ref[...], sig_ref[...] = tanh, sig
    table_parts = split(table)
    for ref, value in ((table_t_ref, table), (hidden_t_ref, tanh * sig)):
        upper, lower = split(jnp.transpose(value))
        upper, lower = upper[:, :KEPT], lower[:, :KEPT]
        ref[:, :KEPT], ref[:, KEPT : 2 * KEPT], ref[:, 2 * KEPT :] = upper, upper, lower
    out_parts = split(out_weight_ref[1])
    for block in range(4):
        rows = pl.ds(256 * block, 256)
        cots = split(cot_ref[rows, :])
        cot_parts[0, rows, :], cot_parts[1, rows, :] = cots
        back_ref[rows, :] = dot3(cots, out_parts, NT)

    for at in range(5):

        @pl.when(routes[at][3])
        def _():
            landing = landed.at[routes[at][2] + 1]
            token_copy(at, landing, landing).wait_recv()

    near_move = chosen(384, 256, [lambda at: 128 + at - near, lambda at: 128 + at + near])
    lane = lax.broadcasted_iota(jnp.int32, (128, 128), 1).astype(F32)
    sub = lax.broadcasted_iota(jnp.int32, (128, 128), 0).astype(F32)
    for strand in range(2):
        block = me if strand == 0 else count - 1 - me
        window[0, 8:10, :] = landed[block][2:4].astype(F32)
        window[0, 10:14, :] = landed[block + 1].astype(F32)
        window[0, 14:16, :] = landed[block + 2][0:2].astype(F32)
        own = window[0, 8:16, :]
        moved = dot(beside(window.at[0]), near_move)
        lower, upper = moved[:, :128], moved[:, 128:]
        if strand == 0:
            code = code_of(lower, own, upper, jnp.where)
        else:
            code = code_of(turned(upper), 3.0 - own, turned(lower), jnp.where)
        window[1, 8:16, :] = jnp.where(own == OUTSIDE, float(NONE), code)
        codes = beside(window.at[1])
        sources = far_sources(far, strand)
        across = dot(codes, chosen(384, 384, sources))
        down = dot(chosen_t(384, sources), codes, NT)
        for tap in range(3):
            taps = slice(128 * tap, 128 * tap + 128)
            for row in range(4):
                at = row + 2 if strand == 0 else 5 - row
                places = slice(512 * strand + 128 * row, 512 * strand + 128 * row + 128)
                hot[places, taps] = jnp.where(down[taps, at : at + 1] == lane, 1.0, 0.0).astype(BF16)
                hot_t[KEPT * tap : KEPT * tap + KEPT, places] = jnp.where(
                    across[at : at + 1, taps] == sub[:KEPT], 1.0, 0.0
                ).astype(BF16)

    for block in range(4):
        rows = pl.ds(256 * block, 256)
        mixed = dot2(hot[rows, :], (high[...], low[...]))
        act, gate = jnp.tanh(mixed[:, :HALF]), sigmoid(mixed[:, HALF:])
        hidden = split(act * gate)
        scaled = back_ref[rows, :] * gate
        grad_act = split(scaled * (1.0 - act * act))
        grad_gate = split(scaled * act * (1.0 - gate))
        for part in range(2):
            hidden_parts[part, rows, :] = hidden[part]
            grad_parts[part, rows, :HALF] = grad_act[part]
            grad_parts[part, rows, HALF:] = grad_gate[part]

    core = lax.rem(me, 2)
    chip = lax.div(me, 2)
    twin = me + 1 - 2 * core
    chips = [exclusive(chip, bits) for bits in range(8)]
    partners = [2 * other + core for other in chips]
    order = (7, 5, 6, 4, 2, 3, 1, 0)
    stages = (
        (GATE_PIECE, SENT, part_gate, paired_gate, summed_gate, arrived_gate, gate_ref),
        (OUT_PIECE, OUT_PIECE, part_out, paired_out, summed_out, arrived_out, out_ref),
    )
    first = {}
    source_chip = 7 * core
    is_source = chip == source_chip

    def rows_of(size, device):
        return pl.ds(pl.multiple_of(device * size, 8), size)

    def landing_of(stage, device):
        return stages[stage][6].at[rows_of(stages[stage][1], device)]

    def edge_landing(device):
        return gate_ref.at[pl.ds(pl.multiple_of(device * SENT + GATE_PIECE, 8), EDGE_PIECE)]

    def edge_copy(at):
        return pltpu.make_async_remote_copy(
            src_ref=part_edge.at[rows_of(EDGE_PIECE, chips[at])],
            dst_ref=edge_landing(partners[at]),
            send_sem=edge_sems.at[0],
            recv_sem=edge_sems.at[1],
            device_id={"seq": partners[at]},
            device_id_type=MESH,
        )

    def pair(stage):
        size, _, part, paired, _, _, _ = stages[stage]
        for at in order:
            source = part.at[rows_of(size, 2 * chips[at] + 1 - core)]
            first[stage, at] = remote(
                source, paired.at[at], sent_sems.at[stage], pair_sems.at[8 * stage + at], twin
            )
            first[stage, at].start()

    def scatter(stage):
        size, _, part, paired, summed, arrived, _ = stages[stage]
        for at in order:
            first[stage, at].wait_recv()
            summed[at] = paired[at] + part[rows_of(size, partners[at]), :]
            if at:
                remote(
                    summed.at[at], arrived.at[at], sent_sems.at[2 + stage], chip_sems.at[stage], partners[at]
                ).start()

    def spread(stage):
        size, sent, _, _, summed, arrived, out = stages[stage]
        whole = arrived.at[pl.ds(1, 7)]
        remote(whole, whole, sent_sems.at[2 + stage], chip_sems.at[stage], twin).wait_recv()
        total = summed[0]
        for at in order[:-1]:
            total = total + arrived[at]
        out[pl.ds(pl.multiple_of(me * sent, 8), size), :] = total
        mine = landing_of(stage, me)
        for at in order[:-1]:
            remote(
                mine, mine, sent_sems.at[4 + stage], spread_sems.at[8 * stage + at], partners[at]
            ).start()
        remote(mine, mine, sent_sems.at[6 + stage], twin_sems.at[stage], twin).start()

    def forward(stage):
        for at in order[:-1]:
            landing = landing_of(stage, partners[at])
            remote(
                landing, landing, sent_sems.at[4 + stage], spread_sems.at[8 * stage + at], partners[at]
            ).wait_recv()
            remote(landing, landing, sent_sems.at[6 + stage], twin_sems.at[stage], twin).start()

    def finish(stage):
        size, sent, part, _, _, _, out = stages[stage]
        whole = out.at[pl.ds(0, 8 * sent)]
        remote(whole, whole, sent_sems.at[6 + stage], twin_sems.at[stage], twin).wait_recv()
        for step, (ref, rows) in enumerate(((part, 8 * size), (part, 7 * size), (out, 7 * sent), (out, 8 * sent))):
            view = ref.at[pl.ds(0, rows)]
            remote(view, view, sent_sems.at[2 * step + stage], twin_sems.at[stage], twin).wait_send()

    cot_pair = (cot_parts[0], cot_parts[1])
    sums = dot2(hot_t[...], (grad_parts[0], grad_parts[1]))
    cot_sums = dot2(hot_t[KEPT : 2 * KEPT, :], cot_pair)
    columns = [
        sums[KEPT * tap : KEPT * tap + KEPT, 128 * at : 128 * at + 128] for tap in range(3) for at in range(4)
    ] + [cot_sums[:, :128], cot_sums[:, 128:]]
    for at, column in enumerate(columns):
        part_gate[INNER * at : INNER * at + INNER, :] = column[:INNER]
    pair(0)
    for at, column in enumerate(columns):
        part_edge[EDGE * at : EDGE * at + EDGE, :] = jnp.where(
            me == 0, column[INNER : INNER + EDGE], column[INNER + EDGE :]
        )

    @pl.when(is_source)
    def _():
        for at in order[:-1]:
            edge_copy(at).start()
        own_rows = pl.ds(pl.multiple_of(me * SENT + GATE_PIECE, 8), EDGE_PIECE)
        gate_ref[own_rows, :] = part_edge[rows_of(EDGE_PIECE, chip), :]

    product = dot3((hidden_parts[0], hidden_parts[1]), cot_pair, TN)
    part_out[:HALF, :], part_out[HALF:, :] = product[:, :128], product[:, 128:]
    scatter(0)
    pair(1)
    scatter(1)
    for block in range(4):
        rows = pl.ds(256 * block, 256)
        result_ref[rows, :] = dot2(hot[rows, ROWS : 2 * ROWS], table_parts) + dot3(
            (hidden_parts[0, rows, :], hidden_parts[1, rows, :]), out_parts
        )
    for layer in range(2):
        for at in range(4):
            parts = split(conv_ref[layer, at] if at < 3 else mix_ref[layer])
            for part in range(2):
                weight_parts_ref[layer, at, part] = parts[part]
    parts = split(out_weight_ref[0])
    for part in range(2):
        out_parts_ref[part] = parts[part]

    @pl.when(jnp.logical_not(is_source))
    def _():
        edge_copy(0).wait_recv()

    spread(0)
    spread(1)
    forward(0)
    forward(1)
    finish(0)
    finish(1)
    for at in range(5):

        @pl.when(routes[at][1])
        def _():
            token_copy(at, tokens_hbm, landed.at[me + 1]).wait_send()

    @pl.when(is_source)
    def _():
        view = part_edge.at[pl.ds(0, 7 * EDGE_PIECE)]
        remote(view, view, edge_sems.at[0], edge_sems.at[1], twin).wait_send()


def main(tokens, dilations, embed, conv, mix, bias, out_weight, cot_fwd, cot_rev, picks, swap, count):
    length = cot_fwd.shape[0]
    shape = lambda *dims: jax.ShapeDtypeStruct(dims, F32)
    like = lambda array: pltpu.VMEM(array.shape, array.dtype)
    sems = pltpu.SemaphoreType.DMA
    return pl.pallas_call(
        main_kernel,
        out_shape=[
            shape(count * SENT, 128),
            shape(count * OUT_PIECE, 128),
            shape(2 * length, HALF),
            jax.ShapeDtypeStruct((HALF, 3 * KEPT), BF16),
            jax.ShapeDtypeStruct((HALF, 3 * KEPT), BF16),
            shape(ROWS, HALF),
            shape(ROWS, HALF),
            jax.ShapeDtypeStruct((2, 4, 2, HALF, 2 * HALF), BF16),
            jax.ShapeDtypeStruct((2, HALF, HALF), BF16),
        ],
        in_specs=[HBM] * 11,
        out_specs=[VMEM] * 9,
        scratch_shapes=[
            pltpu.SMEM(dilations.shape, jnp.int32),
            like(embed),
            like(conv),
            like(mix),
            like(bias),
            like(out_weight),
            pltpu.VMEM((2 * length, HALF), F32),
            like(picks),
            like(swap),
            pltpu.VMEM((count + 2,) + tokens.shape, jnp.int32),
            pltpu.VMEM((2, 24, 128), F32),
            pltpu.VMEM((24, 2 * HALF), F32),
            pltpu.VMEM((3 * ROWS, 2 * HALF), BF16),
            pltpu.VMEM((3 * ROWS, 2 * HALF), BF16),
            pltpu.VMEM((2 * length, 3 * ROWS), BF16),
            pltpu.VMEM((3 * KEPT, 2 * length), BF16),
            pltpu.VMEM((2, 2 * length, HALF), BF16),
            pltpu.VMEM((2, 2 * length, HALF), BF16),
            pltpu.VMEM((2, 2 * length, 2 * HALF), BF16),
            pltpu.VMEM((2 * length, HALF), F32),
            pltpu.VMEM((count * GATE_PIECE, 128), F32),
            pltpu.VMEM((count * OUT_PIECE, 128), F32),
            pltpu.VMEM((8 * EDGE_PIECE, 128), F32),
        ]
        + [pltpu.VMEM((8, size, 128), F32) for _ in range(3) for size in (GATE_PIECE, OUT_PIECE)]
        + [
            sems((11,)),
            sems((2, 5)),
            sems((8,)),
            sems((16,)),
            sems((2,)),
            sems((16,)),
            sems((2,)),
            sems((2,)),
        ],
        compiler_params=pltpu.CompilerParams(
            collective_id=0, has_side_effects=True, vmem_limit_bytes=40 << 20
        ),
        name="local_work_and_sums",
    )(
        *[
            pltpu.with_memory_space_constraint(array, pltpu.HBM)
            for array in (
                tokens, dilations, embed, conv, mix, bias, out_weight, cot_fwd, cot_rev, picks, swap
            )
        ]
    )


def pieces_of(begin, rows, piece, place):
    at = begin
    while at < begin + rows:
        device, inside = at // piece, at % piece
        length = min(piece - inside, begin + rows - at)
        yield at - begin, place(device) + inside, length
        at += length


def gradient_kernel(
    gate_ref,
    out_ref,
    result_ref,
    table_t_ref,
    hidden_t_ref,
    tanh_ref,
    sig_ref,
    weight_parts_ref,
    out_parts_ref,
    embed_ref,
    picks_t_ref,
    swap_ref,
    out_fwd_hbm,
    out_rev_hbm,
    grad_embed_hbm,
    grad_conv_hbm,
    grad_mix_hbm,
    grad_bias_hbm,
    grad_out_hbm,
    grad_embed_ref,
    grad_conv_ref,
    grad_mix_ref,
    grad_bias_ref,
    grad_out_ref,
    sums,
    wide,
    rows_left,
    rows_right,
    sems,
):
    length = out_fwd_hbm.shape[0]
    stores = []

    def store(source, landing):
        stores.append(pltpu.make_async_copy(source, landing, sems.at[len(stores)]))
        stores[-1].start()

    store(result_ref.at[pl.ds(0, length)], out_fwd_hbm)
    store(result_ref.at[pl.ds(length, length)], out_rev_hbm)
    for at in range(2):
        store(out_ref.at[pl.ds(HALF * at, HALF)], grad_out_hbm.at[1, :, pl.ds(128 * at, 128)])
    for at in range(14):
        tap, columns = at // 4, pl.ds(128 * (at % 4), 128)
        runs = list(pieces_of(INNER * at, INNER, GATE_PIECE, lambda device: SENT * device))
        for side in range(2):
            for offset, address, size in pieces_of(
                EDGE * at, EDGE, EDGE_PIECE, lambda chip: SENT * (2 * chip + side) + GATE_PIECE
            ):
                runs.append((INNER + EDGE * side + offset, address, size))
        for offset, address, size in runs:
            sums[tap, pl.ds(offset, size), columns] = gate_ref[pl.ds(address, size), :]
    grad_bias_ref[1:2, :] = jnp.sum(sums[1], axis=0, keepdims=True)

    swap = swap_ref[:KEPT, :KEPT]
    grad = sums[3, :, :HALF]
    parts = [split(sums[tap]) for tap in range(3)]
    parts.append([dot(swap, part).astype(BF16) for part in parts[1]])
    table_t = table_t_ref[...]
    for at in range(4):
        upper, lower = parts[at]
        product = dot(table_t, jnp.concatenate([upper, lower, upper], axis=0))
        if at < 3:
            grad_conv_ref[1, at] = product
            store(grad_conv_ref.at[1, at], grad_conv_hbm.at[1, at])
        else:
            grad_mix_ref[1] = product
            store(grad_mix_ref.at[1], grad_mix_hbm.at[1])
        grad = grad + dot3(parts[at], (weight_parts_ref[1, at, 0], weight_parts_ref[1, at, 1]), NT)

    grads = split(grad)
    tanh, sig = tanh_ref[:KEPT, :], sig_ref[:KEPT, :]
    back = dot3(grads, (out_parts_ref[0], out_parts_ref[1]), NT) * sig
    act, gate = back * (1.0 - tanh * tanh), back * tanh * (1.0 - sig)
    picks_t = picks_t_ref[:, :KEPT]
    wide[:, :HALF] = dot2(picks_t, split(act))
    wide[:, HALF:] = dot2(picks_t, split(gate))
    bases = split(embed_ref[...])
    rows_left[...] = jnp.zeros_like(rows_left)
    rows_right[...] = jnp.zeros_like(rows_right)
    pieces = [split(wide[4 * at : 4 * at + 4, :]) for at in range(4)]
    for at, part in enumerate((0, 0, 1)):
        rows_left[4 * at : 4 * at + 4, :] = bases[part].astype(F32)
    for at, part in enumerate((0, 1, 0)):
        for tap in range(4):
            rows_right[4 * at : 4 * at + 4, 512 * tap : 512 * tap + 512] = pieces[tap][part].astype(F32)
    left = rows_left[...].astype(BF16)
    for at in range(4):
        product = dot(left, rows_right[:, 512 * at : 512 * at + 512].astype(BF16), TN)
        if at < 3:
            grad_conv_ref[0, at] = product
            store(grad_conv_ref.at[0, at], grad_conv_hbm.at[0, at])
        else:
            grad_mix_ref[0] = product
            store(grad_mix_ref.at[0], grad_mix_hbm.at[0])
    grad_out_ref[...] = dot(hidden_t_ref[...], jnp.concatenate([grads[0], grads[1], grads[0]], axis=0))
    store(grad_out_ref, grad_out_hbm.at[0])
    grad_bias_ref[0:1, :HALF] = jnp.sum(act, axis=0, keepdims=True)
    grad_bias_ref[0:1, HALF:] = jnp.sum(gate, axis=0, keepdims=True)
    store(grad_bias_ref, grad_bias_hbm)
    embed_grad = dot2(picks_t, grads)[4:8]
    for at in range(4):
        embed_grad = embed_grad + dot3(pieces[at], (weight_parts_ref[0, at, 0], weight_parts_ref[0, at, 1]), NT)
    grad_embed_ref[...] = embed_grad
    store(grad_embed_ref, grad_embed_hbm)
    for copy in stores:
        copy.wait()


def gradients(sums, embed, conv, mix, bias, out_weight, picks_t, swap):
    half_result = jax.ShapeDtypeStruct((sums[2].shape[0] // 2, HALF), F32)
    likes = (embed, conv, mix, bias, out_weight)
    return pl.pallas_call(
        gradient_kernel,
        out_shape=[half_result] * 2 + [jax.ShapeDtypeStruct(like.shape, F32) for like in likes],
        in_specs=[VMEM] * 12,
        out_specs=[HBM] * 7,
        scratch_shapes=[pltpu.VMEM(like.shape, F32) for like in likes[:4]]
        + [
            pltpu.VMEM((HALF, HALF), F32),
            pltpu.VMEM((4, KEPT, 2 * HALF), F32),
            pltpu.VMEM((16, 2 * HALF), F32),
            pltpu.VMEM((16, HALF), F32),
            pltpu.VMEM((16, 8 * HALF), F32),
            pltpu.SemaphoreType.DMA((15,)),
        ],
        compiler_params=pltpu.CompilerParams(vmem_limit_bytes=24 << 20),
        name="gradients",
    )(*sums, embed, picks_t, swap)


def on_device(
    tokens, dilations, embed, conv_weight, mix_weight, gate_bias, out_weight, cot_fwd, cot_rev
):
    count = lax.axis_size("seq")
    picks, picks_t, swap = [jnp.asarray(value, BF16) for value in selectors()]
    weights = (embed, conv_weight, mix_weight, gate_bias, out_weight)
    sums = main(
        tokens.reshape(tokens.shape[0] // 128, 128), dilations, *weights, cot_fwd, cot_rev, picks, swap, count
    )
    return tuple(gradients(sums, *weights, picks_t, swap))


def solution(mesh):
    in_specs = (
        P(("dp", "seq")),
        P(),
        P(),
        P(),
        P(),
        P(),
        P(),
        P(("dp", "seq"), None),
        P(("dp", "seq"), None),
    )
    out_specs = (
        P(("dp", "seq"), None),
        P(("dp", "seq"), None),
        P("dp", None),
        P("dp", None, None, None),
        P("dp", None, None),
        P("dp", None),
        P("dp", None, None),
    )
    return jax.shard_map(
        on_device, mesh=mesh, in_specs=in_specs, out_specs=out_specs, check_vma=False
    )
```
